32 devices in a mesh: illum: 2 (over y), gx: 4 (over x, core), gy: 4 (over z).
Axes of the slice: x: 2, y: 2, z: 4, core: 2. Of those that a mesh axis runs over, the one named last changes fastest.
Arguments:
- density: float32 [128, 64, 128], P('gx', 'gy'), may hold values from 0 to 1
- moment_one: float32 [128, 64, 128], P('gx', 'gy'), may hold values from -0.6 to 0.6
- moment_two: float32 [128, 64, 128], P('gx', 'gy'), may hold values from 0.0002 to 0.0006
- forward_field: bfloat16 [2, 2, 3, 128, 64, 128], P('illum', None, None, 'gx', 'gy'), may hold values from -6 to 6
- adjoint_field: bfloat16 [2, 2, 3, 128, 64, 128], P('illum', None, None, 'gx', 'gy'), may hold values from -6 to 6
- objective_weight: float32 [2], P('illum'), may hold values from 0.02 to 0.2
Outputs:
- new_density: float32 [128, 64, 128], P('gx', 'gy')
- new_moment_one: float32 [128, 64, 128], P('gx', 'gy')
- new_moment_two: float32 [128, 64, 128], P('gx', 'gy')
- physical: float32 [128, 64, 128], P('gx', 'gy')
The draws below stay inside these ranges and needn't reach their ends.
All inputs are finite; a program needn't handle non-finite values.
Results may differ from the reference program's by a relative error of at most 0.0003.
Values sent between devices are 32-bit elements; how exact they have to be, the bound alone decides.
A program may use at most 64 MiB of HBM per device.

```python
import math
import jax
import jax.numpy as jnp
from jax import lax

RADIUS = 8
SOURCES = 2
NX = 128
NY = 64
NZ = 128


def level_of(stream_key, shape, cuts, smallest, largest):
    gain, own = 1.0, jax.random.fold_in(stream_key, 6)
    for dim, shards_of in cuts:
        heights = jnp.exp(jax.random.uniform(jax.random.fold_in(own, dim), (shards_of,), jnp.float32, smallest / len(cuts), largest / len(cuts)))
        gain = gain * jnp.repeat(heights, shape[dim] // shards_of).reshape([-1 if axis == dim else 1 for axis in range(len(shape))])
    return gain


def normal_values(own_key, dims, width, most, split=(), kind=jnp.bfloat16):
    array = width * jax.random.normal(own_key, dims, jnp.float32)
    if split:
        array = array * level_of(own_key, dims, split, -0.22, 0.18)
    return jnp.clip(array, -most, most).astype(kind)


def setup_inputs(seed: int = 0) -> dict:
    key_list = jax.random.split(jax.random.key(seed), 7)
    return {
        "density": jnp.clip(1.0 * jax.random.uniform(key_list[0], (NX, NY, NZ), jnp.float32) ** level_of(key_list[0], (NX, NY, NZ), ((0, 4), (1, 4)), -0.2, 0.2), 0.0, 1.0),
        "moment_one": jnp.clip(jax.random.uniform(key_list[1], (NX, NY, NZ), jnp.float32, -0.6, 0.6) * level_of(key_list[1], (NX, NY, NZ), ((0, 4), (1, 4)), -0.4, 0.0), -0.6, 0.6),
        "moment_two": jnp.clip(jnp.exp(math.log(0.0006) - 1.09861236 * jax.random.uniform(key_list[2], (NX, NY, NZ), jnp.float32) ** level_of(key_list[2], (NX, NY, NZ), ((0, 4), (1, 4)), -0.2, 0.2)), 0.0002, 0.0006),
        "forward_field": normal_values(key_list[3], (SOURCES, 2, 3, NX, NY, NZ), 1.0, 6.0, ((0, 2), (3, 4), (4, 4))),
        "adjoint_field": normal_values(key_list[4], (SOURCES, 2, 3, NX, NY, NZ), 1.0, 6.0, ((0, 2), (3, 4), (4, 4))),
        "objective_weight": jnp.clip(jnp.exp(math.log(0.2) - 2.3025851 * jax.random.uniform(key_list[5], (SOURCES,), jnp.float32) ** level_of(key_list[5], (SOURCES,), ((0, 2),), -0.2, 0.2)), 0.02, 0.2),
    }


sharpness = 8.0
threshold = 0.5

def tap_weights():
    offsets = jnp.arange(-RADIUS, RADIUS + 1)
    return ((RADIUS + 1 - jnp.abs(offsets)) / (RADIUS + 1) ** 2).astype(jnp.float32)

def band_matrix(length):
    rows = jnp.arange(length)[:, None]
    cols = jnp.arange(length)[None, :]
    apart = jnp.abs(rows - cols)
    values = (RADIUS + 1 - apart).astype(jnp.float32) / float((RADIUS + 1) ** 2)
    return jnp.where(apart <= RADIUS, values, jnp.float32(0.0))

def line_filter(padded, axis, length):
    weights = tap_weights()
    total = jnp.zeros(padded.shape[:axis] + (length,) + padded.shape[axis + 1:], jnp.float32)
    for offset in range(2 * RADIUS + 1):
        total = total + weights[offset] * lax.slice_in_dim(padded, offset, offset + length, axis=axis)
    return total

def depth_filter(field):
    shape = field.shape
    flat = field.reshape(-1, shape[2])
    out = jnp.dot(flat, band_matrix(shape[2]), precision=lax.Precision.HIGHEST, preferred_element_type=jnp.float32)
    return out.reshape(shape)

def full_filter(field):
    padded = jnp.pad(field, ((RADIUS, RADIUS), (RADIUS, RADIUS), (0, 0)))
    along_x = line_filter(padded, 0, field.shape[0])
    along_y = line_filter(along_x, 1, field.shape[1])
    return depth_filter(along_y)

def project(value):
    scale = jnp.tanh(sharpness * threshold) + jnp.tanh(sharpness * (1.0 - threshold))
    return (jnp.tanh(sharpness * threshold) + jnp.tanh(sharpness * (value - threshold))) / scale

def slope(value):
    scale = jnp.tanh(sharpness * threshold) + jnp.tanh(sharpness * (1.0 - threshold))
    inner = jnp.tanh(sharpness * (value - threshold))
    return sharpness * (1.0 - inner * inner) / scale

def reference(density, moment_one, moment_two, forward_field, adjoint_field, objective_weight):
    filtered = full_filter(density)

    def one_source(items):
        fwd, adj, weight = items
        fwd = fwd.astype(jnp.float32)
        adj = adj.astype(jnp.float32)
        intersection = lax.optimization_barrier(jnp.sum(fwd[0] * adj[0] - fwd[1] * adj[1], axis=0))
        return weight * intersection
    terms = lax.map(one_source, (forward_field, adjoint_field, objective_weight))
    sensitivity = lax.optimization_barrier(jnp.sum(terms, axis=0))
    chained = sensitivity * slope(filtered)
    gradient = full_filter(chained)
    new_moment_one = 0.9 * moment_one + 0.1 * gradient
    new_moment_two = 0.999 * moment_two + 0.001 * gradient * gradient
    first_fix = 1.0 - 0.9 ** 5
    second_fix = 1.0 - 0.999 ** 5
    step = new_moment_one / first_fix / (jnp.sqrt(new_moment_two / second_fix) + 1e-08)
    new_density = jnp.clip(density - 0.05 * step, 0.0, 1.0)
    physical = project(full_filter(new_density))
    return (new_density, new_moment_one, new_moment_two, physical)
```

```python
import functools
import math

import jax
import jax.numpy as jnp
from jax import lax
from jax.experimental import pallas as pl
from jax.experimental.pallas import tpu as pltpu
from jax.sharding import PartitionSpec as P

RADIUS = 8
SHARPNESS = 8.0
THRESHOLD = 0.5
TANH_EDGE = math.tanh(SHARPNESS * THRESHOLD)
SCALE = math.tanh(SHARPNESS * THRESHOLD) + math.tanh(SHARPNESS * (1.0 - THRESHOLD))
NORM = 1.0 / float((RADIUS + 1) ** 6)
FIRST_FIX = 1.0 / (1.0 - 0.9**5)
SECOND_FIX = 1.0 / (1.0 - 0.999**5)
MESH = pl.DeviceIdType.MESH
ROUNDS = 3


def split(value):
    high = value.astype(jnp.bfloat16)
    low = (value - high.astype(jnp.float32)).astype(jnp.bfloat16)
    return high, low


def box(value):
    n = value.shape[0]
    two = value[: n - 1] + value[1:]
    four = two[: n - 3] + two[2:]
    eight = four[: n - 7] + four[4:]
    return eight[: n - 8] + value[8:]


def depth_matrix(length):
    row = lax.broadcasted_iota(jnp.int32, (2 * length, length), 0)
    col = lax.broadcasted_iota(jnp.int32, (2 * length, length), 1)
    row = jnp.where(row >= length, row - length, row)
    taps = jnp.maximum(RADIUS + 1 - jnp.abs(row - col), 0)
    return taps.astype(jnp.float32).astype(jnp.bfloat16)


def kernel(
    sizes,
    den,
    m1,
    m2,
    fwd,
    adj,
    weight,
    new_den,
    new_m1,
    new_m2,
    physical,
    ubuf,
    xbuf,
    sens,
    fbuf,
    abuf,
    m1buf,
    m2buf,
    local_sem,
    y_send,
    y_recv,
    t_send,
    t_recv,
    x_send,
    x_recv,
    s_send,
    s_recv,
):
    n_illum, n_gx, n_gy = sizes
    tile_x, tile_y, depth = den.shape
    sources, _, comps = fwd.shape[:3]
    groups = tile_x // RADIUS
    me = lax.axis_index("illum")
    gx = lax.axis_index("gx")
    gy = lax.axis_index("gy")
    odd = lax.rem(gx, 2)
    even = 1 - odd
    reach = tile_x - RADIUS
    starts = [even * (reach - 2 * RADIUS * j) + RADIUS * j for j in range(groups)]
    own = pl.ds(RADIUS, tile_y)

    loads = {}

    def load(name, src, dst):
        copy = pltpu.make_async_copy(src, dst, local_sem.at[len(loads)])
        copy.start()
        loads[name] = copy

    for j in range(groups):
        part = pl.ds(starts[j], RADIUS)
        load(("f", j), fwd.at[:, :, :, part], fbuf.at[:, :, :, part])
        load(("a", j), adj.at[:, :, :, part], abuf.at[:, :, :, part])
    load("d", den, ubuf.at[0, pl.ds(0, tile_x), own])
    load("m1", m1, m1buf)
    load("m2", m2, m2buf)

    pair = gx + even - odd
    beyond = gx - even + odd
    has_pair = jnp.logical_and(pair >= 0, pair < n_gx)
    has_beyond = jnp.logical_and(beyond >= 0, beyond < n_gx)
    pair = jnp.clip(pair, 0, n_gx - 1)
    beyond = jnp.clip(beyond, 0, n_gx - 1)
    y_there = (gy > 0, gy < n_gy - 1)
    y_at = (jnp.maximum(gy - 1, 0), jnp.minimum(gy + 1, n_gy - 1))
    y_device = [{"gy": at} for at in y_at]
    c_there = [jnp.logical_and(has_beyond, there) for there in y_there]
    c_device = [{"gx": beyond, "gy": at} for at in y_at]
    others = [{"illum": lax.rem(me + k, n_illum)} for k in range(1, n_illum)]

    barrier = pltpu.get_barrier_semaphore()
    greeted = [
        (y_there[0], y_device[0]),
        (y_there[1], y_device[1]),
        (has_pair, {"gx": pair}),
        (has_beyond, {"gx": beyond}),
        (c_there[0], c_device[0]),
        (c_there[1], c_device[1]),
    ]
    for there, device in greeted:

        @pl.when(there)
        def _(device=device):
            pl.semaphore_signal(barrier, inc=1, device_id=device, device_id_type=MESH)

    for device in others:
        pl.semaphore_signal(barrier, inc=1, device_id=device, device_id_type=MESH)

    for there, land in ((y_there[0], 0), (y_there[1], RADIUS + tile_y)):

        @pl.when(jnp.logical_not(there))
        def _(land=land):
            for r in range(ROUNDS):
                ubuf[r, :, pl.ds(land, RADIUS)] = jnp.zeros(
                    (tile_x + RADIUS, RADIUS, depth), jnp.float32
                )

    pair_land = even * (tile_x + RADIUS)
    beyond_land = odd * (tile_x + RADIUS)
    for there, land in ((has_pair, pair_land), (has_beyond, beyond_land)):

        @pl.when(jnp.logical_not(there))
        def _(land=land):
            for r in range(ROUNDS):
                xbuf[r, pl.ds(land, RADIUS)] = jnp.zeros(
                    (RADIUS, tile_y, depth), jnp.float32
                )

    z_taps = depth_matrix(depth)

    peers = jnp.int32(len(others))
    for there, _ in greeted:
        peers = peers + there.astype(jnp.int32)
    pl.semaphore_wait(barrier, peers)

    sent_rows = (RADIUS, tile_y)
    landing = (RADIUS + tile_y, 0)

    def rows_of(r, j, low, n, source):
        part = pl.ds(starts[j], RADIUS)
        if source is None:
            return ubuf.at[r, part, pl.ds(low, n)]
        return source.at[part, pl.ds(low - RADIUS, n)]

    def y_copy(r, d, j, source=None):
        return pltpu.make_async_remote_copy(
            src_ref=rows_of(r, j, sent_rows[d], RADIUS, source),
            dst_ref=ubuf.at[r, pl.ds(starts[j], RADIUS), pl.ds(landing[d], RADIUS)],
            send_sem=y_send.at[r, d, j],
            recv_sem=y_recv.at[r, d, j],
            device_id=y_device[d],
            device_id_type=MESH,
        )

    last = groups - 1

    def corner_copy(r, d, source=None):
        return pltpu.make_async_remote_copy(
            src_ref=rows_of(r, last, sent_rows[d], RADIUS, source),
            dst_ref=ubuf.at[r, pl.ds(tile_x, RADIUS), pl.ds(landing[d], RADIUS)],
            send_sem=t_send.at[r, d],
            recv_sem=t_recv.at[r, d],
            device_id=c_device[d],
            device_id_type=MESH,
        )

    def beyond_copy(r, source=None):
        return pltpu.make_async_remote_copy(
            src_ref=rows_of(r, last, RADIUS, tile_y, source),
            dst_ref=ubuf.at[r, pl.ds(tile_x, RADIUS), own],
            send_sem=t_send.at[r, 2],
            recv_sem=t_recv.at[r, 2],
            device_id={"gx": beyond},
            device_id_type=MESH,
        )

    def pair_copy(r, land):
        return pltpu.make_async_remote_copy(
            src_ref=xbuf.at[r, pl.ds(RADIUS + starts[0], RADIUS)],
            dst_ref=xbuf.at[r, pl.ds(land, RADIUS)],
            send_sem=x_send.at[r],
            recv_sem=x_recv.at[r],
            device_id={"gx": pair},
            device_id_type=MESH,
        )

    def s_copy(k, j, slot):
        part = pl.ds(starts[j], RADIUS)
        return pltpu.make_async_remote_copy(
            src_ref=sens.at[me, part],
            dst_ref=sens.at[slot, part],
            send_sem=s_send.at[k, j],
            recv_sem=s_recv.at[k, j],
            device_id=others[k],
            device_id_type=MESH,
        )

    def send(r, j, source=None):
        if j == last:
            for d in (0, 1):

                @pl.when(c_there[d])
                def _(d=d):
                    corner_copy(r, d, source).start()

            @pl.when(has_beyond)
            def _():
                beyond_copy(r, source).start()

        for d in (0, 1):

            @pl.when(y_there[d])
            def _(d=d):
                y_copy(r, d, j, source).start()

    for j in (last, *range(last)):
        send(0, j, den)

    for j in range(groups):
        loads["f", j].wait()
        loads["a", j].wait()
        for i in range(RADIUS):
            q = starts[j] + i
            total = None
            for s in range(sources):
                real = None
                for c in range(comps):
                    a = fbuf[s, 0, c, q].astype(jnp.float32) * abuf[s, 0, c, q].astype(
                        jnp.float32
                    )
                    b = fbuf[s, 1, c, q].astype(jnp.float32) * abuf[s, 1, c, q].astype(
                        jnp.float32
                    )
                    real = (a - b) if real is None else real + (a - b)
                term = weight[s] * real
                total = term if total is None else total + term
            sens[me, q] = total
        for k in range(len(others)):
            s_copy(k, j, me).start()

    def filter_rows(r, start, out):
        total = None
        for k in range(RADIUS + 1):
            row = ubuf[r, pl.ds(start, RADIUS), pl.ds(k, tile_y)]
            if k < RADIUS:
                row = row + ubuf[r, pl.ds(start, RADIUS), pl.ds(2 * RADIUS - k, tile_y)]
            row = row * float(k + 1)
            total = row if total is None else total + row
        xbuf[r, pl.ds(out, RADIUS)] = total

    def y_filter(r, j):
        for d, there in ((0, y_there[1]), (1, y_there[0])):

            @pl.when(there)
            def _(d=d):
                y_copy(r, d, j).wait_recv()

        filter_rows(r, starts[j], RADIUS + starts[j])
        if j == 0:

            @pl.when(has_pair)
            def _():
                pair_copy(r, odd * (tile_x + RADIUS)).start()

    def pair_arrive(r):
        @pl.when(has_pair)
        def _():
            pair_copy(r, pair_land).wait_recv()

    def beyond_filter(r):
        for d in (0, 1):

            @pl.when(c_there[1 - d])
            def _(d=d):
                corner_copy(r, d).wait_recv()

        @pl.when(has_beyond)
        def _():
            beyond_copy(r).wait_recv()
            filter_rows(r, tile_x, beyond_land)

    def xz_filter(r, j):
        value = xbuf[r, pl.ds(starts[j], 3 * RADIUS)]
        value = box(box(value)).reshape(RADIUS * tile_y, depth)
        both = jnp.concatenate(split(value), axis=1)
        out = jnp.dot(both, z_taps, preferred_element_type=jnp.float32)
        return (out * NORM).reshape(RADIUS, tile_y, depth)

    def chain(j, filtered):
        part = pl.ds(starts[j], RADIUS)
        for k in range(len(others)):
            s_copy(k, j, lax.rem(me + n_illum - 1 - k, n_illum)).wait_recv()
        total = sens[0, part]
        for e in range(1, n_illum):
            total = total + sens[e, part]
        inner = jnp.tanh(SHARPNESS * (filtered - THRESHOLD))
        ubuf[1, part, own] = total * (SHARPNESS * (1.0 - inner * inner) * (1.0 / SCALE))
        send(1, j)

    def update(j, gradient):
        part = pl.ds(starts[j], RADIUS)
        one = 0.9 * m1buf[part] + 0.1 * gradient
        two = 0.999 * m2buf[part] + 0.001 * gradient * gradient
        step = one * FIRST_FIX / (jnp.sqrt(two * SECOND_FIX) + 1e-08)
        value = jnp.clip(ubuf[0, part, own] - 0.05 * step, 0.0, 1.0)
        ubuf[2, part, own] = value
        send(2, j)
        new_m1[part] = one
        new_m2[part] = two
        new_den[part] = value

    def finish(j, value):
        part = pl.ds(starts[j], RADIUS)
        physical[part] = (TANH_EDGE + jnp.tanh(SHARPNESS * (value - THRESHOLD))) * (
            1.0 / SCALE
        )

    loads["d"].wait()
    for r, point in enumerate((chain, update, finish)):
        if r == 1:
            loads["m1"].wait()
            loads["m2"].wait()
        y_filter(r, 0)
        y_filter(r, 1)
        pair_arrive(r)
        point(0, xz_filter(r, 0))
        for j in range(2, groups):
            y_filter(r, j)
            point(j - 1, xz_filter(r, j - 1))
        beyond_filter(r)
        point(last, xz_filter(r, last))

    for j in range(groups):
        for k in range(len(others)):
            s_copy(k, j, me).wait_send()
    for r in range(ROUNDS):
        source = den if r == 0 else None
        for d in (0, 1):

            @pl.when(y_there[d])
            def _(d=d):
                for j in range(groups):
                    y_copy(r, d, j, source).wait_send()

            @pl.when(c_there[d])
            def _(d=d):
                corner_copy(r, d, source).wait_send()

        @pl.when(has_beyond)
        def _():
            beyond_copy(r, source).wait_send()

        @pl.when(has_pair)
        def _():
            pair_copy(r, odd * (tile_x + RADIUS)).wait_send()


def export(a, b, c, d, a_out, b_out, c_out, d_out, sem):
    copies = [
        pltpu.make_async_copy(src, dst, sem.at[i])
        for i, (src, dst) in enumerate(
            ((a, a_out), (b, b_out), (c, c_out), (d, d_out))
        )
    ]
    for copy in copies:
        copy.start()
    for copy in copies:
        copy.wait()


def shards(sizes, density, moment_one, moment_two, forward_field, adjoint_field, objective_weight):
    tile_x, tile_y, depth = density.shape
    n_illum = sizes[0]
    tile = jax.ShapeDtypeStruct(density.shape, jnp.float32)
    f32 = jnp.float32
    far = max(n_illum - 1, 1)
    groups = tile_x // RADIUS
    arguments = [
        pltpu.with_memory_space_constraint(x, pltpu.HBM)
        for x in (density, moment_one, moment_two, forward_field, adjoint_field)
    ]
    results = pl.pallas_call(
        functools.partial(kernel, sizes),
        out_shape=(pltpu.VMEM(density.shape, f32),) * 4,
        in_specs=[pl.BlockSpec(memory_space=pltpu.HBM)] * 5
        + [pl.BlockSpec(memory_space=pltpu.SMEM)],
        out_specs=(pl.BlockSpec(memory_space=pltpu.VMEM),) * 4,
        scratch_shapes=[
            pltpu.VMEM(
                (ROUNDS, tile_x + RADIUS, tile_y + 2 * RADIUS, depth), f32
            ),
            pltpu.VMEM((ROUNDS, tile_x + 2 * RADIUS, tile_y, depth), f32),
            pltpu.VMEM((n_illum, tile_x, tile_y, depth), f32),
            pltpu.VMEM(forward_field.shape, forward_field.dtype),
            pltpu.VMEM(adjoint_field.shape, adjoint_field.dtype),
            pltpu.VMEM(density.shape, f32),
            pltpu.VMEM(density.shape, f32),
            pltpu.SemaphoreType.DMA((2 * groups + 3,)),
            pltpu.SemaphoreType.DMA((ROUNDS, 2, groups)),
            pltpu.SemaphoreType.DMA((ROUNDS, 2, groups)),
            pltpu.SemaphoreType.DMA((ROUNDS, 3)),
            pltpu.SemaphoreType.DMA((ROUNDS, 3)),
            pltpu.SemaphoreType.DMA((ROUNDS,)),
            pltpu.SemaphoreType.DMA((ROUNDS,)),
            pltpu.SemaphoreType.DMA((far, groups)),
            pltpu.SemaphoreType.DMA((far, groups)),
        ],
        compiler_params=pltpu.CompilerParams(
            collective_id=0, has_side_effects=True, vmem_limit_bytes=48 << 20
        ),
        name="design_update",
    )(*arguments, objective_weight)
    return pl.pallas_call(
        export,
        out_shape=(tile,) * 4,
        in_specs=[pl.BlockSpec(memory_space=pltpu.VMEM)] * 4,
        out_specs=(pl.BlockSpec(memory_space=pl.ANY),) * 4,
        scratch_shapes=[pltpu.SemaphoreType.DMA((4,))],
        compiler_params=pltpu.CompilerParams(vmem_limit_bytes=4 << 20),
        name="export_results",
    )(*results)


def solution(mesh):
    field = P("illum", None, None, "gx", "gy", None)
    tile = P("gx", "gy", None)
    sizes = (mesh.shape["illum"], mesh.shape["gx"], mesh.shape["gy"])
    return jax.shard_map(
        functools.partial(shards, sizes),
        mesh=mesh,
        in_specs=(tile, tile, tile, field, field, P("illum")),
        out_specs=(tile,) * 4,
        check_vma=False,
    )
```

```python
import functools
import math

import jax
import jax.numpy as jnp
from jax import lax
from jax.experimental import pallas as pl
from jax.experimental.pallas import tpu as pltpu
from jax.sharding import PartitionSpec as P

RADIUS = 8
SHARPNESS = 8.0
THRESHOLD = 0.5
TANH_EDGE = math.tanh(SHARPNESS * THRESHOLD)
SCALE = math.tanh(SHARPNESS * THRESHOLD) + math.tanh(SHARPNESS * (1.0 - THRESHOLD))
NORM = 1.0 / float((RADIUS + 1) ** 6)
FIRST_FIX = 1.0 / (1.0 - 0.9**5)
SECOND_FIX = 1.0 / (1.0 - 0.999**5)
MESH = pl.DeviceIdType.MESH
ROUNDS = 3
FIRST = (0, 1, 3, 2)
SENS = (0, 1, 2, 3)
LATE = (1, 2, 3)
ORDERS = (
    (("y", 0), ("late", 0), ("y", 1), ("pair", 0), ("out", 0), ("y", 2), ("out", 1), ("y", 3), ("out", 2), ("beyond", 0), ("out", 3), ),
    (("y", 0), ("y", 1), ("pair", 0), ("out", 0), ("y", 2), ("out", 1), ("y", 3), ("out", 2), ("beyond", 0), ("out", 3), ),
    (("y", 0), ("y", 1), ("pair", 0), ("out", 0), ("y", 2), ("out", 1), ("y", 3), ("out", 2), ("beyond", 0), ("out", 3), ),
)


def split(value):
    high = value.astype(jnp.bfloat16)
    low = (value - high.astype(jnp.float32)).astype(jnp.bfloat16)
    return high, low


def box(value):
    n = value.shape[0]
    two = value[: n - 1] + value[1:]
    four = two[: n - 3] + two[2:]
    eight = four[: n - 7] + four[4:]
    return eight[: n - 8] + value[8:]


def depth_matrix(length):
    row = lax.broadcasted_iota(jnp.int32, (2 * length, length), 0)
    col = lax.broadcasted_iota(jnp.int32, (2 * length, length), 1)
    row = jnp.where(row >= length, row - length, row)
    taps = jnp.maximum(RADIUS + 1 - jnp.abs(row - col), 0)
    return taps.astype(jnp.float32).astype(jnp.bfloat16)


def kernel(
    sizes,
    den,
    m1,
    m2,
    fwd,
    adj,
    weight,
    new_den,
    new_m1,
    new_m2,
    physical,
    ubuf,
    xbuf,
    sens,
    fbuf,
    abuf,
    m1buf,
    m2buf,
    local_sem,
    y_send,
    y_recv,
    t_send,
    t_recv,
    x_send,
    x_recv,
    s_send,
    s_recv,
):
    n_illum, n_gx, n_gy = sizes
    tile_x, tile_y, depth = den.shape
    sources, _, comps = fwd.shape[:3]
    groups = tile_x // RADIUS
    me = lax.axis_index("illum")
    gx = lax.axis_index("gx")
    gy = lax.axis_index("gy")
    odd = lax.rem(gx, 2)
    even = 1 - odd
    reach = tile_x - RADIUS
    starts = [even * (reach - 2 * RADIUS * j) + RADIUS * j for j in range(groups)]
    own = pl.ds(RADIUS, tile_y)

    loads = {}

    def load(name, src, dst):
        copy = pltpu.make_async_copy(src, dst, local_sem.at[len(loads)])
        copy.start()
        loads[name] = copy

    for j in range(groups):
        part = pl.ds(starts[j], RADIUS)
        load(("f", j), fwd.at[:, :, :, part], fbuf.at[:, :, :, part])
        load(("a", j), adj.at[:, :, :, part], abuf.at[:, :, :, part])
    load("d", den, ubuf.at[0, pl.ds(0, tile_x), own])
    load("m1", m1, m1buf)
    load("m2", m2, m2buf)

    pair = gx + even - odd
    beyond = gx - even + odd
    has_pair = jnp.logical_and(pair >= 0, pair < n_gx)
    has_beyond = jnp.logical_and(beyond >= 0, beyond < n_gx)
    pair = jnp.clip(pair, 0, n_gx - 1)
    beyond = jnp.clip(beyond, 0, n_gx - 1)
    y_there = (gy > 0, gy < n_gy - 1)
    y_at = (jnp.maximum(gy - 1, 0), jnp.minimum(gy + 1, n_gy - 1))
    y_device = [{"gy": at} for at in y_at]
    c_there = [jnp.logical_and(has_beyond, there) for there in y_there]
    c_device = [{"gx": beyond, "gy": at} for at in y_at]
    others = [{"illum": lax.rem(me + k, n_illum)} for k in range(1, n_illum)]

    barrier = pltpu.get_barrier_semaphore()
    greeted = [
        (y_there[0], y_device[0]),
        (y_there[1], y_device[1]),
        (has_pair, {"gx": pair}),
        (has_beyond, {"gx": beyond}),
        (c_there[0], c_device[0]),
        (c_there[1], c_device[1]),
    ]
    for there, device in greeted:

        @pl.when(there)
        def _(device=device):
            pl.semaphore_signal(barrier, inc=1, device_id=device, device_id_type=MESH)

    for device in others:
        pl.semaphore_signal(barrier, inc=1, device_id=device, device_id_type=MESH)

    for there, land in ((y_there[0], 0), (y_there[1], RADIUS + tile_y)):

        @pl.when(jnp.logical_not(there))
        def _(land=land):
            for r in range(ROUNDS):
                ubuf[r, :, pl.ds(land, RADIUS)] = jnp.zeros(
                    (tile_x + RADIUS, RADIUS, depth), jnp.float32
                )

    pair_land = even * (tile_x + RADIUS)
    beyond_land = odd * (tile_x + RADIUS)
    for there, land in ((has_pair, pair_land), (has_beyond, beyond_land)):

        @pl.when(jnp.logical_not(there))
        def _(land=land):
            for r in range(ROUNDS):
                xbuf[r, pl.ds(land, RADIUS)] = jnp.zeros(
                    (RADIUS, tile_y, depth), jnp.float32
                )

    z_taps = depth_matrix(depth)

    peers = jnp.int32(len(others))
    for there, _ in greeted:
        peers = peers + there.astype(jnp.int32)
    pl.semaphore_wait(barrier, peers)

    sent_rows = (RADIUS, tile_y)
    landing = (RADIUS + tile_y, 0)

    def rows_of(r, j, low, n, source):
        part = pl.ds(starts[j], RADIUS)
        if source is None:
            return ubuf.at[r, part, pl.ds(low, n)]
        return source.at[part, pl.ds(low - RADIUS, n)]

    def y_copy(r, d, j, source=None):
        return pltpu.make_async_remote_copy(
            src_ref=rows_of(r, j, sent_rows[d], RADIUS, source),
            dst_ref=ubuf.at[r, pl.ds(starts[j], RADIUS), pl.ds(landing[d], RADIUS)],
            send_sem=y_send.at[r, d, j],
            recv_sem=y_recv.at[r, d, j],
            device_id=y_device[d],
            device_id_type=MESH,
        )

    last = groups - 1

    def corner_copy(r, d, source=None):
        return pltpu.make_async_remote_copy(
            src_ref=rows_of(r, last, sent_rows[d], RADIUS, source),
            dst_ref=ubuf.at[r, pl.ds(tile_x, RADIUS), pl.ds(landing[d], RADIUS)],
            send_sem=t_send.at[r, d],
            recv_sem=t_recv.at[r, d],
            device_id=c_device[d],
            device_id_type=MESH,
        )

    def beyond_copy(r, source=None):
        return pltpu.make_async_remote_copy(
            src_ref=rows_of(r, last, RADIUS, tile_y, source),
            dst_ref=ubuf.at[r, pl.ds(tile_x, RADIUS), own],
            send_sem=t_send.at[r, 2],
            recv_sem=t_recv.at[r, 2],
            device_id={"gx": beyond},
            device_id_type=MESH,
        )

    def pair_copy(r, land):
        return pltpu.make_async_remote_copy(
            src_ref=xbuf.at[r, pl.ds(RADIUS + starts[0], RADIUS)],
            dst_ref=xbuf.at[r, pl.ds(land, RADIUS)],
            send_sem=x_send.at[r],
            recv_sem=x_recv.at[r],
            device_id={"gx": pair},
            device_id_type=MESH,
        )

    def s_copy(k, j, slot):
        part = pl.ds(starts[j], RADIUS)
        return pltpu.make_async_remote_copy(
            src_ref=sens.at[me, part],
            dst_ref=sens.at[slot, part],
            send_sem=s_send.at[k, j],
            recv_sem=s_recv.at[k, j],
            device_id=others[k],
            device_id_type=MESH,
        )

    def send(r, j, source=None):
        for d in (0, 1):

            @pl.when(y_there[d])
            def _(d=d):
                y_copy(r, d, j, source).start()

        if j == last:
            for d in (0, 1):

                @pl.when(c_there[d])
                def _(d=d):
                    corner_copy(r, d, source).start()

            @pl.when(has_beyond)
            def _():
                beyond_copy(r, source).start()

    for j in FIRST:
        send(0, j, den)

    for j in SENS:
        loads["f", j].wait()
        loads["a", j].wait()
        for i in range(RADIUS):
            q = starts[j] + i
            total = None
            for s in range(sources):
                real = None
                for c in range(comps):
                    a = fbuf[s, 0, c, q].astype(jnp.float32) * abuf[s, 0, c, q].astype(
                        jnp.float32
                    )
                    b = fbuf[s, 1, c, q].astype(jnp.float32) * abuf[s, 1, c, q].astype(
                        jnp.float32
                    )
                    real = (a - b) if real is None else real + (a - b)
                term = weight[s] * real
                total = term if total is None else total + term
            sens[me, q] = total
        if j in LATE:

            @pl.when(odd == 0)
            def _(j=j):
                for k in range(len(others)):
                    s_copy(k, j, me).start()

        else:
            for k in range(len(others)):
                s_copy(k, j, me).start()

    def filter_rows(r, start, out):
        total = None
        for k in range(RADIUS + 1):
            row = ubuf[r, pl.ds(start, RADIUS), pl.ds(k, tile_y)]
            if k < RADIUS:
                row = row + ubuf[r, pl.ds(start, RADIUS), pl.ds(2 * RADIUS - k, tile_y)]
            row = row * float(k + 1)
            total = row if total is None else total + row
        xbuf[r, pl.ds(out, RADIUS)] = total

    def y_filter(r, j):
        for d, there in ((0, y_there[1]), (1, y_there[0])):

            @pl.when(there)
            def _(d=d):
                y_copy(r, d, j).wait_recv()

        filter_rows(r, starts[j], RADIUS + starts[j])
        if j == 0:

            @pl.when(has_pair)
            def _():
                pair_copy(r, odd * (tile_x + RADIUS)).start()

    def pair_arrive(r):
        @pl.when(has_pair)
        def _():
            pair_copy(r, pair_land).wait_recv()

    def beyond_filter(r):
        for d in (0, 1):

            @pl.when(c_there[1 - d])
            def _(d=d):
                corner_copy(r, d).wait_recv()

        @pl.when(has_beyond)
        def _():
            beyond_copy(r).wait_recv()
            filter_rows(r, tile_x, beyond_land)

    def xz_filter(r, j):
        value = xbuf[r, pl.ds(starts[j], 3 * RADIUS)]
        value = box(box(value)).reshape(RADIUS * tile_y, depth)
        both = jnp.concatenate(split(value), axis=1)
        out = jnp.dot(both, z_taps, preferred_element_type=jnp.float32)
        return (out * NORM).reshape(RADIUS, tile_y, depth)

    def chain(j, filtered):
        part = pl.ds(starts[j], RADIUS)
        for k in range(len(others)):
            s_copy(k, j, lax.rem(me + n_illum - 1 - k, n_illum)).wait_recv()
        total = sens[0, part]
        for e in range(1, n_illum):
            total = total + sens[e, part]
        inner = jnp.tanh(SHARPNESS * (filtered - THRESHOLD))
        ubuf[1, part, own] = total * (SHARPNESS * (1.0 - inner * inner) * (1.0 / SCALE))
        send(1, j)

    def update(j, gradient):
        part = pl.ds(starts[j], RADIUS)
        one = 0.9 * m1buf[part] + 0.1 * gradient
        two = 0.999 * m2buf[part] + 0.001 * gradient * gradient
        step = one * FIRST_FIX / (jnp.sqrt(two * SECOND_FIX) + 1e-08)
        value = jnp.clip(ubuf[0, part, own] - 0.05 * step, 0.0, 1.0)
        ubuf[2, part, own] = value
        send(2, j)
        new_m1[part] = one
        new_m2[part] = two
        new_den[part] = value

    def finish(j, value):
        part = pl.ds(starts[j], RADIUS)
        physical[part] = (TANH_EDGE + jnp.tanh(SHARPNESS * (value - THRESHOLD))) * (
            1.0 / SCALE
        )

    loads["d"].wait()
    for r, point in enumerate((chain, update, finish)):
        if r == 1:
            loads["m1"].wait()
            loads["m2"].wait()
        for step, j in ORDERS[r]:
            if step == "y":
                y_filter(r, j)
            elif step == "pair":
                pair_arrive(r)
            elif step == "beyond":
                beyond_filter(r)
            elif step == "late":

                @pl.when(odd == 1)
                def _():
                    for j in LATE:
                        for k in range(len(others)):
                            s_copy(k, j, me).start()

            else:
                point(j, xz_filter(r, j))

    for j in range(groups):
        for k in range(len(others)):
            s_copy(k, j, me).wait_send()
    for r in range(ROUNDS):
        source = den if r == 0 else None
        for d in (0, 1):

            @pl.when(y_there[d])
            def _(d=d):
                for j in range(groups):
                    y_copy(r, d, j, source).wait_send()

            @pl.when(c_there[d])
            def _(d=d):
                corner_copy(r, d, source).wait_send()

        @pl.when(has_beyond)
        def _():
            beyond_copy(r, source).wait_send()

        @pl.when(has_pair)
        def _():
            pair_copy(r, odd * (tile_x + RADIUS)).wait_send()


def export(a, b, c, d, a_out, b_out, c_out, d_out, sem):
    copies = [
        pltpu.make_async_copy(src, dst, sem.at[i])
        for i, (src, dst) in enumerate(
            ((a, a_out), (b, b_out), (c, c_out), (d, d_out))
        )
    ]
    for copy in copies:
        copy.start()
    for copy in copies:
        copy.wait()


def shards(sizes, density, moment_one, moment_two, forward_field, adjoint_field, objective_weight):
    tile_x, tile_y, depth = density.shape
    n_illum = sizes[0]
    tile = jax.ShapeDtypeStruct(density.shape, jnp.float32)
    f32 = jnp.float32
    far = max(n_illum - 1, 1)
    groups = tile_x // RADIUS
    arguments = [
        pltpu.with_memory_space_constraint(x, pltpu.HBM)
        for x in (density, moment_one, moment_two, forward_field, adjoint_field)
    ]
    results = pl.pallas_call(
        functools.partial(kernel, sizes),
        out_shape=(pltpu.VMEM(density.shape, f32),) * 4,
        in_specs=[pl.BlockSpec(memory_space=pltpu.HBM)] * 5
        + [pl.BlockSpec(memory_space=pltpu.SMEM)],
        out_specs=(pl.BlockSpec(memory_space=pltpu.VMEM),) * 4,
        scratch_shapes=[
            pltpu.VMEM(
                (ROUNDS, tile_x + RADIUS, tile_y + 2 * RADIUS, depth), f32
            ),
            pltpu.VMEM((ROUNDS, tile_x + 2 * RADIUS, tile_y, depth), f32),
            pltpu.VMEM((n_illum, tile_x, tile_y, depth), f32),
            pltpu.VMEM(forward_field.shape, forward_field.dtype),
            pltpu.VMEM(adjoint_field.shape, adjoint_field.dtype),
            pltpu.VMEM(density.shape, f32),
            pltpu.VMEM(density.shape, f32),
            pltpu.SemaphoreType.DMA((2 * groups + 3,)),
            pltpu.SemaphoreType.DMA((ROUNDS, 2, groups)),
            pltpu.SemaphoreType.DMA((ROUNDS, 2, groups)),
            pltpu.SemaphoreType.DMA((ROUNDS, 3)),
            pltpu.SemaphoreType.DMA((ROUNDS, 3)),
            pltpu.SemaphoreType.DMA((ROUNDS,)),
            pltpu.SemaphoreType.DMA((ROUNDS,)),
            pltpu.SemaphoreType.DMA((far, groups)),
            pltpu.SemaphoreType.DMA((far, groups)),
        ],
        compiler_params=pltpu.CompilerParams(
            collective_id=0, has_side_effects=True, vmem_limit_bytes=48 << 20
        ),
        name="design_update",
    )(*arguments, objective_weight)
    return pl.pallas_call(
        export,
        out_shape=(tile,) * 4,
        in_specs=[pl.BlockSpec(memory_space=pltpu.VMEM)] * 4,
        out_specs=(pl.BlockSpec(memory_space=pl.ANY),) * 4,
        scratch_shapes=[pltpu.SemaphoreType.DMA((4,))],
        compiler_params=pltpu.CompilerParams(vmem_limit_bytes=4 << 20),
        name="export_results",
    )(*results)


def solution(mesh):
    field = P("illum", None, None, "gx", "gy", None)
    tile = P("gx", "gy", None)
    sizes = (mesh.shape["illum"], mesh.shape["gx"], mesh.shape["gy"])
    return jax.shard_map(
        functools.partial(shards, sizes),
        mesh=mesh,
        in_specs=(tile, tile, tile, field, field, P("illum")),
        out_specs=(tile,) * 4,
        check_vma=False,
    )
```

```python
import functools
import math

import jax
import jax.numpy as jnp
from jax import lax
from jax.experimental import pallas as pl
from jax.experimental.pallas import tpu as pltpu
from jax.sharding import PartitionSpec as P

RADIUS = 8
SHARPNESS = 8.0
THRESHOLD = 0.5
TANH_EDGE = math.tanh(SHARPNESS * THRESHOLD)
SCALE = math.tanh(SHARPNESS * THRESHOLD) + math.tanh(SHARPNESS * (1.0 - THRESHOLD))
NORM = 1.0 / float((RADIUS + 1) ** 6)
FIRST_FIX = 1.0 / (1.0 - 0.9**5)
SECOND_FIX = 1.0 / (1.0 - 0.999**5)
MESH = pl.DeviceIdType.MESH
ROUNDS = 3
FIRST = (0, 1, 3, 2)
SENS = (0, 1, 2, 3)
LATE = (1, 2, 3)
ORDERS = (
    (("y", 0), ("late", 0), ("y", 1), ("pair", 0), ("out", 0), ("y", 2), ("out", 1), ("y", 3), ("out", 2), ("beyond", 0), ("out", 3), ),
    (("y", 0), ("y", 1), ("pair", 0), ("out", 0), ("y", 2), ("out", 1), ("y", 3), ("beyond", 0), ("out", 3), ("out", 2), ),
    (("y", 0), ("y", 1), ("y", 2), ("out", 1), ("y", 3), ("out", 2), ("pair", 0), ("out", 0), ("beyond", 0), ("out", 3), ),
)


def split(value):
    high = value.astype(jnp.bfloat16)
    low = (value - high.astype(jnp.float32)).astype(jnp.bfloat16)
    return high, low


def box(value):
    n = value.shape[0]
    two = value[: n - 1] + value[1:]
    four = two[: n - 3] + two[2:]
    eight = four[: n - 7] + four[4:]
    return eight[: n - 8] + value[8:]


def project(value):
    return (TANH_EDGE + jnp.tanh(SHARPNESS * (value - THRESHOLD))) * (1.0 / SCALE)


def xz_rows(value, z_taps):
    n, tile_y, depth = value.shape
    value = box(box(value)).reshape((n - 2 * RADIUS) * tile_y, depth)
    both = jnp.concatenate(split(value), axis=1)
    out = jnp.dot(both, z_taps, preferred_element_type=jnp.float32)
    return (out * NORM).reshape(n - 2 * RADIUS, tile_y, depth)


def depth_matrix(length):
    row = lax.broadcasted_iota(jnp.int32, (2 * length, length), 0)
    col = lax.broadcasted_iota(jnp.int32, (2 * length, length), 1)
    row = jnp.where(row >= length, row - length, row)
    taps = jnp.maximum(RADIUS + 1 - jnp.abs(row - col), 0)
    return taps.astype(jnp.float32).astype(jnp.bfloat16)


def kernel(
    sizes,
    den,
    m1,
    m2,
    fwd,
    adj,
    weight,
    new_den,
    new_m1,
    new_m2,
    physical,
    tail,
    ubuf,
    xbuf,
    sens,
    fbuf,
    abuf,
    m1buf,
    m2buf,
    stage,
    local_sem,
    y_send,
    y_recv,
    t_send,
    t_recv,
    x_send,
    x_recv,
    s_send,
    s_recv,
):
    n_illum, n_gx, n_gy = sizes
    tile_x, tile_y, depth = den.shape
    sources, _, comps = fwd.shape[:3]
    groups = tile_x // RADIUS
    last = groups - 1
    me = lax.axis_index("illum")
    gx = lax.axis_index("gx")
    gy = lax.axis_index("gy")
    odd = lax.rem(gx, 2)
    even = 1 - odd
    reach = tile_x - RADIUS
    starts = [even * (reach - 2 * RADIUS * j) + RADIUS * j for j in range(groups)]
    own = pl.ds(RADIUS, tile_y)

    pair = gx + even - odd
    beyond = gx - even + odd
    has_pair = jnp.logical_and(pair >= 0, pair < n_gx)
    has_beyond = jnp.logical_and(beyond >= 0, beyond < n_gx)
    pair = jnp.clip(pair, 0, n_gx - 1)
    beyond = jnp.clip(beyond, 0, n_gx - 1)
    y_there = (gy > 0, gy < n_gy - 1)
    y_at = (jnp.maximum(gy - 1, 0), jnp.minimum(gy + 1, n_gy - 1))
    y_device = [{"gy": at} for at in y_at]
    c_there = [jnp.logical_and(has_beyond, there) for there in y_there]
    c_device = [{"gx": beyond, "gy": at} for at in y_at]
    others = [{"illum": lax.rem(me + k, n_illum)} for k in range(1, n_illum)]

    barrier = pltpu.get_barrier_semaphore()
    greeted = [
        (y_there[0], y_device[0]),
        (y_there[1], y_device[1]),
        (has_pair, {"gx": pair}),
        (has_beyond, {"gx": beyond}),
        (c_there[0], c_device[0]),
        (c_there[1], c_device[1]),
    ]
    for device in others:
        pl.semaphore_signal(barrier, inc=1, device_id=device, device_id_type=MESH)

    for there, device in greeted:

        @pl.when(there)
        def _(device=device):
            pl.semaphore_signal(barrier, inc=1, device_id=device, device_id_type=MESH)


    loads = {}

    def load(name, src, dst):
        copy = pltpu.make_async_copy(src, dst, local_sem.at[len(loads)])
        copy.start()
        loads[name] = copy

    for j in range(groups):
        part = pl.ds(starts[j], RADIUS)
        load(("f", j), fwd.at[:, :, :, part], fbuf.at[:, :, :, part])
        load(("a", j), adj.at[:, :, :, part], abuf.at[:, :, :, part])
    load("d", den, ubuf.at[0, pl.ds(0, tile_x), own])
    load("m1", m1, m1buf)
    load("m2", m2, m2buf)

    for there, land in ((y_there[0], 0), (y_there[1], RADIUS + tile_y)):

        @pl.when(jnp.logical_not(there))
        def _(land=land):
            for r in range(ROUNDS):
                ubuf[r, :, pl.ds(land, RADIUS)] = jnp.zeros(
                    (tile_x + RADIUS, RADIUS, depth), jnp.float32
                )

    pair_land = even * (tile_x + RADIUS)
    beyond_land = odd * (tile_x + RADIUS)
    for there, land in ((has_pair, pair_land), (has_beyond, beyond_land)):

        @pl.when(jnp.logical_not(there))
        def _(land=land):
            for r in range(ROUNDS):
                xbuf[r, pl.ds(land, RADIUS)] = jnp.zeros(
                    (RADIUS, tile_y, depth), jnp.float32
                )

    tail_at = {last: RADIUS, last - 1: 2 * RADIUS * even, groups: 2 * RADIUS * odd}

    @pl.when(jnp.logical_not(has_beyond))
    def _():
        tail[pl.ds(tail_at[groups], RADIUS)] = jnp.zeros(
            (RADIUS, tile_y, depth), jnp.float32
        )

    z_taps = depth_matrix(depth)

    peers = jnp.int32(len(others))
    for there, _ in greeted:
        peers = peers + there.astype(jnp.int32)
    pl.semaphore_wait(barrier, peers)

    sent_rows = (RADIUS, tile_y)
    landing = (RADIUS + tile_y, 0)

    def rows_of(r, j, low, n, source):
        part = pl.ds(starts[j], RADIUS)
        if source is None:
            return ubuf.at[r, part, pl.ds(low, n)]
        return source.at[part, pl.ds(low - RADIUS, n)]

    def y_copy(r, d, j, source=None):
        return pltpu.make_async_remote_copy(
            src_ref=rows_of(r, j, sent_rows[d], RADIUS, source),
            dst_ref=ubuf.at[r, pl.ds(starts[j], RADIUS), pl.ds(landing[d], RADIUS)],
            send_sem=y_send.at[r, d, j],
            recv_sem=y_recv.at[r, d, j],
            device_id=y_device[d],
            device_id_type=MESH,
        )

    def corner_copy(r, d, source=None):
        return pltpu.make_async_remote_copy(
            src_ref=rows_of(r, last, sent_rows[d], RADIUS, source),
            dst_ref=ubuf.at[r, pl.ds(tile_x, RADIUS), pl.ds(landing[d], RADIUS)],
            send_sem=t_send.at[r, d],
            recv_sem=t_recv.at[r, d],
            device_id=c_device[d],
            device_id_type=MESH,
        )

    def beyond_copy(r, source=None):
        return pltpu.make_async_remote_copy(
            src_ref=rows_of(r, last, RADIUS, tile_y, source),
            dst_ref=ubuf.at[r, pl.ds(tile_x, RADIUS), own],
            send_sem=t_send.at[r, 2],
            recv_sem=t_recv.at[r, 2],
            device_id={"gx": beyond},
            device_id_type=MESH,
        )

    def pair_copy(r, land):
        return pltpu.make_async_remote_copy(
            src_ref=xbuf.at[r, pl.ds(RADIUS + starts[0], RADIUS)],
            dst_ref=xbuf.at[r, pl.ds(land, RADIUS)],
            send_sem=x_send.at[r],
            recv_sem=x_recv.at[r],
            device_id={"gx": pair},
            device_id_type=MESH,
        )

    def s_copy(k, j, slot):
        part = pl.ds(starts[j], RADIUS)
        return pltpu.make_async_remote_copy(
            src_ref=sens.at[me, part],
            dst_ref=sens.at[slot, part],
            send_sem=s_send.at[k, j],
            recv_sem=s_recv.at[k, j],
            device_id=others[k],
            device_id_type=MESH,
        )

    def send(r, j, source=None):
        if j == last:
            for d in (0, 1):

                @pl.when(c_there[d])
                def _(d=d):
                    corner_copy(r, d, source).start()

        for d in (0, 1):

            @pl.when(y_there[d])
            def _(d=d):
                y_copy(r, d, j, source).start()

        if j == last:

            @pl.when(has_beyond)
            def _():
                beyond_copy(r, source).start()

    for j in FIRST:
        send(0, j, den)

    for j in SENS:
        loads["f", j].wait()
        loads["a", j].wait()
        for i in range(RADIUS):
            q = starts[j] + i
            total = None
            for s in range(sources):
                real = None
                for c in range(comps):
                    a = fbuf[s, 0, c, q].astype(jnp.float32) * abuf[s, 0, c, q].astype(
                        jnp.float32
                    )
                    b = fbuf[s, 1, c, q].astype(jnp.float32) * abuf[s, 1, c, q].astype(
                        jnp.float32
                    )
                    real = (a - b) if real is None else real + (a - b)
                term = weight[s] * real
                total = term if total is None else total + term
            sens[me, q] = total
        if j in LATE:

            @pl.when(odd == 0)
            def _(j=j):
                for k in range(len(others)):
                    s_copy(k, j, me).start()

        else:
            for k in range(len(others)):
                s_copy(k, j, me).start()

    def taps(ref, step, n):
        one, two, three, four, five = (
            ref[:, pl.ds(step * k, n)] for k in range(5)
        )
        return (one + five) + 2.0 * (two + four) + 3.0 * three

    def store(r, out, j, total):
        if r == ROUNDS - 1 and j in tail_at:
            tail[pl.ds(tail_at[j], RADIUS)] = total
        if r < ROUNDS - 1 or j <= last:
            xbuf[r, pl.ds(out, RADIUS)] = total

    def filter_rows(r, start, out, j):
        near = pl.ds(0, tile_y + 12)
        stage[:, near] = taps(ubuf.at[r, pl.ds(start, RADIUS)], 1, tile_y + 12)
        total = taps(stage, 3, tile_y)
        store(r, out, j, total)

    def y_filter(r, j):
        for d, there in ((0, y_there[1]), (1, y_there[0])):

            @pl.when(there)
            def _(d=d):
                y_copy(r, d, j).wait_recv()

        filter_rows(r, starts[j], RADIUS + starts[j], j)
        if j == 0:

            @pl.when(has_pair)
            def _():
                pair_copy(r, odd * (tile_x + RADIUS)).start()

    def pair_arrive(r):
        @pl.when(has_pair)
        def _():
            pair_copy(r, pair_land).wait_recv()

    def beyond_filter(r):
        for d in (0, 1):

            @pl.when(c_there[1 - d])
            def _(d=d):
                corner_copy(r, d).wait_recv()

        @pl.when(has_beyond)
        def _():
            beyond_copy(r).wait_recv()
            filter_rows(r, tile_x, beyond_land, groups)

    def xz_filter(r, j):
        return xz_rows(xbuf[r, pl.ds(starts[j], 3 * RADIUS)], z_taps)

    def chain(j, filtered):
        part = pl.ds(starts[j], RADIUS)
        for k in range(len(others)):
            s_copy(k, j, lax.rem(me + n_illum - 1 - k, n_illum)).wait_recv()
        total = sens[0, part]
        for e in range(1, n_illum):
            total = total + sens[e, part]
        inner = jnp.tanh(SHARPNESS * (filtered - THRESHOLD))
        ubuf[1, part, own] = total * (SHARPNESS * (1.0 - inner * inner) * (1.0 / SCALE))
        send(1, j)

    def update(j, gradient):
        part = pl.ds(starts[j], RADIUS)
        one = 0.9 * m1buf[part] + 0.1 * gradient
        two = 0.999 * m2buf[part] + 0.001 * gradient * gradient
        step = one * FIRST_FIX / (jnp.sqrt(two * SECOND_FIX) + 1e-08)
        value = jnp.clip(ubuf[0, part, own] - 0.05 * step, 0.0, 1.0)
        ubuf[2, part, own] = value
        send(2, j)
        new_m1[part] = one
        new_m2[part] = two
        new_den[part] = value

    def finish(j, value):
        part = pl.ds(starts[j], RADIUS)
        physical[part] = project(value)

    loads["d"].wait()
    for r, point in enumerate((chain, update, finish)):
        if r == 1:
            loads["m1"].wait()
            loads["m2"].wait()
        for step, j in ORDERS[r]:
            if step == "y":
                y_filter(r, j)
            elif step == "pair":
                pair_arrive(r)
            elif step == "beyond":
                beyond_filter(r)
            elif step == "late":

                @pl.when(odd == 1)
                def _():
                    for j in LATE:
                        for k in range(len(others)):
                            s_copy(k, j, me).start()

            elif r < ROUNDS - 1 or j < last:
                point(j, xz_filter(r, j))

    for j in range(groups):
        for k in range(len(others)):
            s_copy(k, j, me).wait_send()
    for r in range(ROUNDS):
        source = den if r == 0 else None
        for d in (0, 1):

            @pl.when(y_there[d])
            def _(d=d):
                for j in range(groups):
                    y_copy(r, d, j, source).wait_send()

            @pl.when(c_there[d])
            def _(d=d):
                corner_copy(r, d, source).wait_send()

        @pl.when(has_beyond)
        def _():
            beyond_copy(r, source).wait_send()

        @pl.when(has_pair)
        def _():
            pair_copy(r, odd * (tile_x + RADIUS)).wait_send()


def export(a, b, c, d, tail, a_out, b_out, c_out, d_out, edge, sem):
    tile_x = d.shape[0]
    even = 1 - lax.rem(lax.axis_index("gx"), 2)
    done = pl.ds(RADIUS * even, tile_x - RADIUS)
    copies = [
        pltpu.make_async_copy(src, dst, sem.at[i])
        for i, (src, dst) in enumerate(
            ((d.at[done], d_out.at[done]), (a, a_out), (b, b_out), (c, c_out))
        )
    ]
    for copy in copies:
        copy.start()
    edge[...] = project(xz_rows(tail[...], depth_matrix(d.shape[2])))
    final = pltpu.make_async_copy(
        edge, d_out.at[pl.ds((tile_x - RADIUS) * (1 - even), RADIUS)], sem.at[4]
    )
    final.start()
    for copy in (*copies, final):
        copy.wait()


def shards(sizes, density, moment_one, moment_two, forward_field, adjoint_field, objective_weight):
    tile_x, tile_y, depth = density.shape
    n_illum = sizes[0]
    tile = jax.ShapeDtypeStruct(density.shape, jnp.float32)
    f32 = jnp.float32
    far = max(n_illum - 1, 1)
    groups = tile_x // RADIUS
    arguments = [
        pltpu.with_memory_space_constraint(x, pltpu.HBM)
        for x in (density, moment_one, moment_two, forward_field, adjoint_field)
    ]
    results = pl.pallas_call(
        functools.partial(kernel, sizes),
        out_shape=(pltpu.VMEM(density.shape, f32),) * 4
        + (pltpu.VMEM((3 * RADIUS, tile_y, depth), f32),),
        in_specs=[pl.BlockSpec(memory_space=pltpu.HBM)] * 5
        + [pl.BlockSpec(memory_space=pltpu.SMEM)],
        out_specs=(pl.BlockSpec(memory_space=pltpu.VMEM),) * 5,
        scratch_shapes=[
            pltpu.VMEM(
                (ROUNDS, tile_x + RADIUS, tile_y + 2 * RADIUS, depth), f32
            ),
            pltpu.VMEM((ROUNDS, tile_x + 2 * RADIUS, tile_y, depth), f32),
            pltpu.VMEM((n_illum, tile_x, tile_y, depth), f32),
            pltpu.VMEM(forward_field.shape, forward_field.dtype),
            pltpu.VMEM(adjoint_field.shape, adjoint_field.dtype),
            pltpu.VMEM(density.shape, f32),
            pltpu.VMEM(density.shape, f32),
            pltpu.VMEM((RADIUS, tile_y + 2 * RADIUS, depth), f32),
            pltpu.SemaphoreType.DMA((2 * groups + 3,)),
            pltpu.SemaphoreType.DMA((ROUNDS, 2, groups)),
            pltpu.SemaphoreType.DMA((ROUNDS, 2, groups)),
            pltpu.SemaphoreType.DMA((ROUNDS, 3)),
            pltpu.SemaphoreType.DMA((ROUNDS, 3)),
            pltpu.SemaphoreType.DMA((ROUNDS,)),
            pltpu.SemaphoreType.DMA((ROUNDS,)),
            pltpu.SemaphoreType.DMA((far, groups)),
            pltpu.SemaphoreType.DMA((far, groups)),
        ],
        compiler_params=pltpu.CompilerParams(
            collective_id=0, has_side_effects=True, vmem_limit_bytes=48 << 20
        ),
        name="design_update",
    )(*arguments, objective_weight)
    return pl.pallas_call(
        export,
        out_shape=(tile,) * 4,
        in_specs=[pl.BlockSpec(memory_space=pltpu.VMEM)] * 5,
        out_specs=(pl.BlockSpec(memory_space=pl.ANY),) * 4,
        scratch_shapes=[
            pltpu.VMEM((RADIUS, tile_y, depth), f32),
            pltpu.SemaphoreType.DMA((5,)),
        ],
        compiler_params=pltpu.CompilerParams(vmem_limit_bytes=4 << 20),
        name="export_results",
    )(*results)


def solution(mesh):
    field = P("illum", None, None, "gx", "gy", None)
    tile = P("gx", "gy", None)
    sizes = (mesh.shape["illum"], mesh.shape["gx"], mesh.shape["gy"])
    return jax.shard_map(
        functools.partial(shards, sizes),
        mesh=mesh,
        in_specs=(tile, tile, tile, field, field, P("illum")),
        out_specs=(tile,) * 4,
        check_vma=False,
    )
```

```python
import functools
import math

import jax
import jax.numpy as jnp
from jax import lax
from jax.experimental import pallas as pl
from jax.experimental.pallas import tpu as pltpu
from jax.sharding import PartitionSpec as P

RADIUS = 8
SHARPNESS = 8.0
THRESHOLD = 0.5
TANH_EDGE = math.tanh(SHARPNESS * THRESHOLD)
SCALE = math.tanh(SHARPNESS * THRESHOLD) + math.tanh(SHARPNESS * (1.0 - THRESHOLD))
NORM = 1.0 / float((RADIUS + 1) ** 6)
FIRST_FIX = 1.0 / (1.0 - 0.9**5)
SECOND_FIX = 1.0 / (1.0 - 0.999**5)
MESH = pl.DeviceIdType.MESH
ROUNDS = 3
LATE_FROM = 1


def plan(groups):
    last = groups - 1
    sweep = [("y", 0), ("y", 1), ("pair", 0), ("out", 0)]
    end = [("y", 0), ("y", 1)]
    for j in range(2, groups):
        sweep += [("y", j), ("out", j - 1)]
        end += [("y", j), ("out", j - 1)]
    first = sweep[:1] + [("late", 0)] + sweep[1:] + [("beyond", 0), ("out", last)]
    second = sweep[:-1] + [("beyond", 0), ("out", last), ("out", last - 1)]
    third = end + [("pair", 0), ("out", 0), ("beyond", 0), ("out", last)]
    return first, second, third


def split(value):
    high = value.astype(jnp.bfloat16)
    low = (value - high.astype(jnp.float32)).astype(jnp.bfloat16)
    return high, low


def box(value):
    n = value.shape[0]
    two = value[: n - 1] + value[1:]
    four = two[: n - 3] + two[2:]
    eight = four[: n - 7] + four[4:]
    return eight[: n - 8] + value[8:]


def project(value):
    return (TANH_EDGE + jnp.tanh(SHARPNESS * (value - THRESHOLD))) * (1.0 / SCALE)


def xz_rows(value, z_taps):
    n, tile_y, depth = value.shape
    value = box(box(value)).reshape((n - 2 * RADIUS) * tile_y, depth)
    both = jnp.concatenate(split(value), axis=1)
    out = jnp.dot(both, z_taps, preferred_element_type=jnp.float32)
    return (out * NORM).reshape(n - 2 * RADIUS, tile_y, depth)


def depth_matrix(length):
    row = lax.broadcasted_iota(jnp.int32, (2 * length, length), 0)
    col = lax.broadcasted_iota(jnp.int32, (2 * length, length), 1)
    row = jnp.where(row >= length, row - length, row)
    taps = jnp.maximum(RADIUS + 1 - jnp.abs(row - col), 0)
    return taps.astype(jnp.float32).astype(jnp.bfloat16)


def kernel(
    sizes,
    den,
    m1,
    m2,
    fwd,
    adj,
    weight,
    new_den,
    new_m1,
    new_m2,
    physical,
    tail,
    z_taps,
    ubuf,
    xbuf,
    sens,
    fbuf,
    abuf,
    m1buf,
    m2buf,
    stage,
    local_sem,
    y_send,
    y_recv,
    t_send,
    t_recv,
    x_send,
    x_recv,
    s_send,
    s_recv,
):
    n_illum, n_gx, n_gy = sizes
    tile_x, tile_y, depth = den.shape
    sources, _, comps = fwd.shape[:3]
    groups = tile_x // RADIUS
    last = groups - 1
    me = lax.axis_index("illum")
    gx = lax.axis_index("gx")
    gy = lax.axis_index("gy")
    odd = lax.rem(gx, 2)
    even = 1 - odd
    reach = tile_x - RADIUS
    starts = [even * (reach - 2 * RADIUS * j) + RADIUS * j for j in range(groups)]
    own = pl.ds(RADIUS, tile_y)

    pair = gx + even - odd
    beyond = gx - even + odd
    has_pair = jnp.logical_and(pair >= 0, pair < n_gx)
    has_beyond = jnp.logical_and(beyond >= 0, beyond < n_gx)
    pair = jnp.clip(pair, 0, n_gx - 1)
    beyond = jnp.clip(beyond, 0, n_gx - 1)
    y_there = (gy > 0, gy < n_gy - 1)
    y_at = (jnp.maximum(gy - 1, 0), jnp.minimum(gy + 1, n_gy - 1))
    y_device = [{"gy": at} for at in y_at]
    c_there = [jnp.logical_and(has_beyond, there) for there in y_there]
    c_device = [{"gx": beyond, "gy": at} for at in y_at]
    others = [{"illum": lax.rem(me + k, n_illum)} for k in range(1, n_illum)]

    barrier = pltpu.get_barrier_semaphore()
    greeted = [
        (y_there[0], y_device[0]),
        (y_there[1], y_device[1]),
        (has_pair, {"gx": pair}),
        (has_beyond, {"gx": beyond}),
        (c_there[0], c_device[0]),
        (c_there[1], c_device[1]),
    ]
    for device in others:
        pl.semaphore_signal(barrier, inc=1, device_id=device, device_id_type=MESH)

    for there, device in greeted:

        @pl.when(there)
        def _(device=device):
            pl.semaphore_signal(barrier, inc=1, device_id=device, device_id_type=MESH)


    loads = {}

    def load(name, src, dst):
        copy = pltpu.make_async_copy(src, dst, local_sem.at[len(loads)])
        copy.start()
        loads[name] = copy

    for j in range(groups):
        part = pl.ds(starts[j], RADIUS)
        load(("f", j), fwd.at[:, :, :, part], fbuf.at[:, :, :, part])
        load(("a", j), adj.at[:, :, :, part], abuf.at[:, :, :, part])
    load("d", den, ubuf.at[0, pl.ds(0, tile_x), own])
    load("m1", m1, m1buf)
    load("m2", m2, m2buf)

    for there, land in ((y_there[0], 0), (y_there[1], RADIUS + tile_y)):

        @pl.when(jnp.logical_not(there))
        def _(land=land):
            for r in range(ROUNDS):
                ubuf[r, :, pl.ds(land, RADIUS)] = jnp.zeros(
                    (tile_x + RADIUS, RADIUS, depth), jnp.float32
                )

    pair_land = even * (tile_x + RADIUS)
    beyond_land = odd * (tile_x + RADIUS)
    for there, land in ((has_pair, pair_land), (has_beyond, beyond_land)):

        @pl.when(jnp.logical_not(there))
        def _(land=land):
            for r in range(ROUNDS):
                xbuf[r, pl.ds(land, RADIUS)] = jnp.zeros(
                    (RADIUS, tile_y, depth), jnp.float32
                )

    tail_at = {last: RADIUS, last - 1: 2 * RADIUS * even, groups: 2 * RADIUS * odd}

    @pl.when(jnp.logical_not(has_beyond))
    def _():
        tail[pl.ds(tail_at[groups], RADIUS)] = jnp.zeros(
            (RADIUS, tile_y, depth), jnp.float32
        )

    z_taps[...] = depth_matrix(depth)

    peers = jnp.int32(len(others))
    for there, _ in greeted:
        peers = peers + there.astype(jnp.int32)
    pl.semaphore_wait(barrier, peers)

    sent_rows = (RADIUS, tile_y)
    landing = (RADIUS + tile_y, 0)

    def rows_of(r, j, low, n, source):
        part = pl.ds(starts[j], RADIUS)
        if source is None:
            return ubuf.at[r, part, pl.ds(low, n)]
        return source.at[part, pl.ds(low - RADIUS, n)]

    def y_copy(r, d, j, source=None):
        return pltpu.make_async_remote_copy(
            src_ref=rows_of(r, j, sent_rows[d], RADIUS, source),
            dst_ref=ubuf.at[r, pl.ds(starts[j], RADIUS), pl.ds(landing[d], RADIUS)],
            send_sem=y_send.at[r, d, j],
            recv_sem=y_recv.at[r, d, j],
            device_id=y_device[d],
            device_id_type=MESH,
        )

    def corner_copy(r, d, source=None):
        return pltpu.make_async_remote_copy(
            src_ref=rows_of(r, last, sent_rows[d], RADIUS, source),
            dst_ref=ubuf.at[r, pl.ds(tile_x, RADIUS), pl.ds(landing[d], RADIUS)],
            send_sem=t_send.at[r, d],
            recv_sem=t_recv.at[r, d],
            device_id=c_device[d],
            device_id_type=MESH,
        )

    def beyond_copy(r, source=None):
        return pltpu.make_async_remote_copy(
            src_ref=rows_of(r, last, RADIUS, tile_y, source),
            dst_ref=ubuf.at[r, pl.ds(tile_x, RADIUS), own],
            send_sem=t_send.at[r, 2],
            recv_sem=t_recv.at[r, 2],
            device_id={"gx": beyond},
            device_id_type=MESH,
        )

    def pair_copy(r, land):
        return pltpu.make_async_remote_copy(
            src_ref=xbuf.at[r, pl.ds(RADIUS + starts[0], RADIUS)],
            dst_ref=xbuf.at[r, pl.ds(land, RADIUS)],
            send_sem=x_send.at[r],
            recv_sem=x_recv.at[r],
            device_id={"gx": pair},
            device_id_type=MESH,
        )

    def s_copy(k, j, slot):
        part = pl.ds(starts[j], RADIUS)
        return pltpu.make_async_remote_copy(
            src_ref=sens.at[me, part],
            dst_ref=sens.at[slot, part],
            send_sem=s_send.at[k, j],
            recv_sem=s_recv.at[k, j],
            device_id=others[k],
            device_id_type=MESH,
        )

    def send(r, j, source=None):
        if j == last:
            for d in (0, 1):

                @pl.when(c_there[d])
                def _(d=d):
                    corner_copy(r, d, source).start()

        for d in (0, 1):

            @pl.when(y_there[d])
            def _(d=d):
                y_copy(r, d, j, source).start()

        if j == last:

            @pl.when(has_beyond)
            def _():
                beyond_copy(r, source).start()

    for j in (0, 1, last, *range(2, last)):
        send(0, j, den)

    for j in range(groups):
        loads["f", j].wait()
        loads["a", j].wait()
        for i in range(RADIUS):
            q = starts[j] + i
            total = None
            for s in range(sources):
                real = None
                for c in range(comps):
                    a = fbuf[s, 0, c, q].astype(jnp.float32) * abuf[s, 0, c, q].astype(
                        jnp.float32
                    )
                    b = fbuf[s, 1, c, q].astype(jnp.float32) * abuf[s, 1, c, q].astype(
                        jnp.float32
                    )
                    real = (a - b) if real is None else real + (a - b)
                term = weight[s] * real
                total = term if total is None else total + term
            sens[me, q] = total
        if j >= LATE_FROM:

            @pl.when(odd == 0)
            def _(j=j):
                for k in range(len(others)):
                    s_copy(k, j, me).start()

        else:
            for k in range(len(others)):
                s_copy(k, j, me).start()

    def taps(ref, step, n):
        one, two, three, four, five = (
            ref[:, pl.ds(step * k, n)] for k in range(5)
        )
        return (one + five) + 2.0 * (two + four) + 3.0 * three

    def store(r, out, j, total):
        if r == ROUNDS - 1 and j in tail_at:
            tail[pl.ds(tail_at[j], RADIUS)] = total
        if r < ROUNDS - 1 or j <= last:
            xbuf[r, pl.ds(out, RADIUS)] = total

    def filter_rows(r, start, out, j):
        near = pl.ds(0, tile_y + 12)
        stage[:, near] = taps(ubuf.at[r, pl.ds(start, RADIUS)], 1, tile_y + 12)
        total = taps(stage, 3, tile_y)
        store(r, out, j, total)

    def y_filter(r, j):
        for d, there in ((0, y_there[1]), (1, y_there[0])):

            @pl.when(there)
            def _(d=d):
                y_copy(r, d, j).wait_recv()

        filter_rows(r, starts[j], RADIUS + starts[j], j)
        if j == 0:

            @pl.when(has_pair)
            def _():
                pair_copy(r, odd * (tile_x + RADIUS)).start()

    def pair_arrive(r):
        @pl.when(has_pair)
        def _():
            pair_copy(r, pair_land).wait_recv()

    def beyond_filter(r):
        for d in (0, 1):

            @pl.when(c_there[1 - d])
            def _(d=d):
                corner_copy(r, d).wait_recv()

        @pl.when(has_beyond)
        def _():
            beyond_copy(r).wait_recv()
            filter_rows(r, tile_x, beyond_land, groups)

    def xz_filter(r, j):
        return xz_rows(xbuf[r, pl.ds(starts[j], 3 * RADIUS)], z_taps[...])

    def chain(j, filtered):
        part = pl.ds(starts[j], RADIUS)
        for k in range(len(others)):
            s_copy(k, j, lax.rem(me + n_illum - 1 - k, n_illum)).wait_recv()
        total = sens[0, part]
        for e in range(1, n_illum):
            total = total + sens[e, part]
        inner = jnp.tanh(SHARPNESS * (filtered - THRESHOLD))
        ubuf[1, part, own] = total * (SHARPNESS * (1.0 - inner * inner) * (1.0 / SCALE))
        send(1, j)

    def update(j, gradient):
        part = pl.ds(starts[j], RADIUS)
        one = 0.9 * m1buf[part] + 0.1 * gradient
        two = 0.999 * m2buf[part] + 0.001 * gradient * gradient
        step = one * FIRST_FIX / (jnp.sqrt(two * SECOND_FIX) + 1e-08)
        value = jnp.clip(ubuf[0, part, own] - 0.05 * step, 0.0, 1.0)
        ubuf[2, part, own] = value
        send(2, j)
        new_m1[part] = one
        new_m2[part] = two
        new_den[part] = value

    def finish(j, value):
        part = pl.ds(starts[j], RADIUS)
        physical[part] = project(value)

    def drain(r):
        source = den if r == 0 else None
        for d in (0, 1):

            @pl.when(y_there[d])
            def _(d=d):
                for j in range(groups):
                    y_copy(r, d, j, source).wait_send()

            @pl.when(c_there[d])
            def _(d=d):
                corner_copy(r, d, source).wait_send()

        @pl.when(has_beyond)
        def _():
            beyond_copy(r, source).wait_send()

        @pl.when(has_pair)
        def _():
            pair_copy(r, odd * (tile_x + RADIUS)).wait_send()

    def drain_early():
        for j in range(groups):
            for k in range(len(others)):
                s_copy(k, j, me).wait_send()
        for r in range(ROUNDS - 1):
            drain(r)

    loads["d"].wait()
    steps = plan(groups)
    for r, point in enumerate((chain, update, finish)):
        if r == 1:
            loads["m1"].wait()
            loads["m2"].wait()
        for step, j in steps[r]:
            if step == "y":
                y_filter(r, j)
            elif step == "pair":
                pair_arrive(r)
            elif step == "beyond":
                if r == ROUNDS - 1:
                    drain_early()
                beyond_filter(r)
            elif step == "late":

                @pl.when(odd == 1)
                def _():
                    for j in range(LATE_FROM, groups):
                        for k in range(len(others)):
                            s_copy(k, j, me).start()

            elif r < ROUNDS - 1 or j < last:
                point(j, xz_filter(r, j))

    drain(ROUNDS - 1)


def export(a, b, c, d, tail, z_taps, a_out, b_out, c_out, d_out, edge, sem):
    tile_x = d.shape[0]
    even = 1 - lax.rem(lax.axis_index("gx"), 2)
    done = pl.ds(RADIUS * even, tile_x - RADIUS)
    copies = [
        pltpu.make_async_copy(src, dst, sem.at[i])
        for i, (src, dst) in enumerate(
            ((d.at[done], d_out.at[done]), (a, a_out), (b, b_out), (c, c_out))
        )
    ]
    for copy in copies:
        copy.start()
    edge[...] = project(xz_rows(tail[...], z_taps[...]))
    final = pltpu.make_async_copy(
        edge, d_out.at[pl.ds((tile_x - RADIUS) * (1 - even), RADIUS)], sem.at[4]
    )
    final.start()
    for copy in (*copies, final):
        copy.wait()


def shards(sizes, density, moment_one, moment_two, forward_field, adjoint_field, objective_weight):
    tile_x, tile_y, depth = density.shape
    n_illum = sizes[0]
    tile = jax.ShapeDtypeStruct(density.shape, jnp.float32)
    f32 = jnp.float32
    far = max(n_illum - 1, 1)
    groups = tile_x // RADIUS
    arguments = [
        pltpu.with_memory_space_constraint(x, pltpu.HBM)
        for x in (density, moment_one, moment_two, forward_field, adjoint_field)
    ]
    results = pl.pallas_call(
        functools.partial(kernel, sizes),
        out_shape=(pltpu.VMEM(density.shape, f32),) * 4
        + (
            pltpu.VMEM((3 * RADIUS, tile_y, depth), f32),
            pltpu.VMEM((2 * depth, depth), jnp.bfloat16),
        ),
        in_specs=[pl.BlockSpec(memory_space=pltpu.HBM)] * 5
        + [pl.BlockSpec(memory_space=pltpu.SMEM)],
        out_specs=(pl.BlockSpec(memory_space=pltpu.VMEM),) * 6,
        scratch_shapes=[
            pltpu.VMEM(
                (ROUNDS, tile_x + RADIUS, tile_y + 2 * RADIUS, depth), f32
            ),
            pltpu.VMEM((ROUNDS, tile_x + 2 * RADIUS, tile_y, depth), f32),
            pltpu.VMEM((n_illum, tile_x, tile_y, depth), f32),
            pltpu.VMEM(forward_field.shape, forward_field.dtype),
            pltpu.VMEM(adjoint_field.shape, adjoint_field.dtype),
            pltpu.VMEM(density.shape, f32),
            pltpu.VMEM(density.shape, f32),
            pltpu.VMEM((RADIUS, tile_y + 2 * RADIUS, depth), f32),
            pltpu.SemaphoreType.DMA((2 * groups + 3,)),
            pltpu.SemaphoreType.DMA((ROUNDS, 2, groups)),
            pltpu.SemaphoreType.DMA((ROUNDS, 2, groups)),
            pltpu.SemaphoreType.DMA((ROUNDS, 3)),
            pltpu.SemaphoreType.DMA((ROUNDS, 3)),
            pltpu.SemaphoreType.DMA((ROUNDS,)),
            pltpu.SemaphoreType.DMA((ROUNDS,)),
            pltpu.SemaphoreType.DMA((far, groups)),
            pltpu.SemaphoreType.DMA((far, groups)),
        ],
        compiler_params=pltpu.CompilerParams(
            collective_id=0, has_side_effects=True, vmem_limit_bytes=48 << 20
        ),
        name="design_update",
    )(*arguments, objective_weight)
    return pl.pallas_call(
        export,
        out_shape=(tile,) * 4,
        in_specs=[pl.BlockSpec(memory_space=pltpu.VMEM)] * 6,
        out_specs=(pl.BlockSpec(memory_space=pl.ANY),) * 4,
        scratch_shapes=[
            pltpu.VMEM((RADIUS, tile_y, depth), f32),
            pltpu.SemaphoreType.DMA((5,)),
        ],
        compiler_params=pltpu.CompilerParams(vmem_limit_bytes=4 << 20),
        name="export_results",
    )(*results)


def solution(mesh):
    field = P("illum", None, None, "gx", "gy", None)
    tile = P("gx", "gy", None)
    sizes = (mesh.shape["illum"], mesh.shape["gx"], mesh.shape["gy"])
    return jax.shard_map(
        functools.partial(shards, sizes),
        mesh=mesh,
        in_specs=(tile, tile, tile, field, field, P("illum")),
        out_specs=(tile,) * 4,
        check_vma=False,
    )
```

```python
import functools
import math

import jax
import jax.numpy as jnp
from jax import lax
from jax.experimental import pallas as pl
from jax.experimental.pallas import tpu as pltpu
from jax.sharding import PartitionSpec as P

RADIUS = 8
SHARPNESS = 8.0
THRESHOLD = 0.5
TANH_EDGE = math.tanh(SHARPNESS * THRESHOLD)
SCALE = math.tanh(SHARPNESS * THRESHOLD) + math.tanh(SHARPNESS * (1.0 - THRESHOLD))
NORM = 1.0 / float((RADIUS + 1) ** 6)
FIRST_FIX = 1.0 / (1.0 - 0.9**5)
SECOND_FIX = 1.0 / (1.0 - 0.999**5)
MESH = pl.DeviceIdType.MESH
ROUNDS = 3
LATE_FROM = 1


def plan(groups):
    last = groups - 1
    sweep = [("y", 0), ("y", 1), ("pair", 0), ("out", 0)]
    end = [("y", 0), ("y", 1)]
    for j in range(2, groups):
        sweep += [("y", j), ("out", j - 1)]
        end += [("y", j), ("out", j - 1)]
    first = sweep[:1] + [("late", 0)] + sweep[1:2] + [("late", 1)] + sweep[2:] + [("beyond", 0), ("out", last)]
    second = sweep[:-1] + [("beyond", 0), ("out", last), ("out", last - 1)]
    third = end + [("pair", 0), ("out", 0), ("beyond", 0), ("out", last)]
    return first, second, third


def split(value):
    high = value.astype(jnp.bfloat16)
    low = (value - high.astype(jnp.float32)).astype(jnp.bfloat16)
    return high, low


def box(value):
    n = value.shape[0]
    two = value[: n - 1] + value[1:]
    four = two[: n - 3] + two[2:]
    eight = four[: n - 7] + four[4:]
    return eight[: n - 8] + value[8:]


def project(value):
    return (TANH_EDGE + jnp.tanh(SHARPNESS * (value - THRESHOLD))) * (1.0 / SCALE)


def xz_rows(value, z_taps):
    n, tile_y, depth = value.shape
    value = box(box(value)).reshape((n - 2 * RADIUS) * tile_y, depth)
    both = jnp.concatenate(split(value), axis=1)
    out = jnp.dot(both, z_taps, preferred_element_type=jnp.float32)
    return (out * NORM).reshape(n - 2 * RADIUS, tile_y, depth)


def depth_matrix(length):
    row = lax.broadcasted_iota(jnp.int32, (2 * length, length), 0)
    col = lax.broadcasted_iota(jnp.int32, (2 * length, length), 1)
    row = jnp.where(row >= length, row - length, row)
    taps = jnp.maximum(RADIUS + 1 - jnp.abs(row - col), 0)
    return taps.astype(jnp.float32).astype(jnp.bfloat16)


def kernel(
    sizes,
    den,
    m1,
    m2,
    fwd,
    adj,
    weight,
    new_den,
    new_m1,
    new_m2,
    physical,
    tail,
    z_taps,
    ubuf,
    xbuf,
    sens,
    fbuf,
    abuf,
    m1buf,
    m2buf,
    stage,
    local_sem,
    y_send,
    y_recv,
    t_send,
    t_recv,
    x_send,
    x_recv,
    s_send,
    s_recv,
):
    n_illum, n_gx, n_gy = sizes
    tile_x, tile_y, depth = den.shape
    sources, _, comps = fwd.shape[:3]
    groups = tile_x // RADIUS
    last = groups - 1
    me = lax.axis_index("illum")
    gx = lax.axis_index("gx")
    gy = lax.axis_index("gy")
    odd = lax.rem(gx, 2)
    even = 1 - odd
    reach = tile_x - RADIUS
    starts = [even * (reach - 2 * RADIUS * j) + RADIUS * j for j in range(groups)]
    own = pl.ds(RADIUS, tile_y)

    pair = gx + even - odd
    beyond = gx - even + odd
    has_pair = jnp.logical_and(pair >= 0, pair < n_gx)
    has_beyond = jnp.logical_and(beyond >= 0, beyond < n_gx)
    pair = jnp.clip(pair, 0, n_gx - 1)
    beyond = jnp.clip(beyond, 0, n_gx - 1)
    y_there = (gy > 0, gy < n_gy - 1)
    y_at = (jnp.maximum(gy - 1, 0), jnp.minimum(gy + 1, n_gy - 1))
    y_device = [{"gy": at} for at in y_at]
    c_there = [jnp.logical_and(has_beyond, there) for there in y_there]
    c_device = [{"gx": beyond, "gy": at} for at in y_at]
    others = [{"illum": lax.rem(me + k, n_illum)} for k in range(1, n_illum)]

    barrier = pltpu.get_barrier_semaphore()
    greeted = [
        (y_there[0], y_device[0]),
        (y_there[1], y_device[1]),
        (has_pair, {"gx": pair}),
        (has_beyond, {"gx": beyond}),
        (c_there[0], c_device[0]),
        (c_there[1], c_device[1]),
    ]
    for device in others:
        pl.semaphore_signal(barrier, inc=1, device_id=device, device_id_type=MESH)

    for there, device in greeted:

        @pl.when(there)
        def _(device=device):
            pl.semaphore_signal(barrier, inc=1, device_id=device, device_id_type=MESH)


    loads = {}

    def load(name, src, dst):
        copy = pltpu.make_async_copy(src, dst, local_sem.at[len(loads)])
        copy.start()
        loads[name] = copy

    for j in range(groups):
        part = pl.ds(starts[j], RADIUS)
        load(("f", j), fwd.at[:, :, :, part], fbuf.at[:, :, :, part])
        load(("a", j), adj.at[:, :, :, part], abuf.at[:, :, :, part])
    load("d", den, ubuf.at[0, pl.ds(0, tile_x), own])
    load("m1", m1, m1buf)
    load("m2", m2, m2buf)

    for there, land in ((y_there[0], 0), (y_there[1], RADIUS + tile_y)):

        @pl.when(jnp.logical_not(there))
        def _(land=land):
            for r in range(ROUNDS):
                ubuf[r, :, pl.ds(land, RADIUS)] = jnp.zeros(
                    (tile_x + RADIUS, RADIUS, depth), jnp.float32
                )

    pair_land = even * (tile_x + RADIUS)
    beyond_land = odd * (tile_x + RADIUS)
    for there, land in ((has_pair, pair_land), (has_beyond, beyond_land)):

        @pl.when(jnp.logical_not(there))
        def _(land=land):
            for r in range(ROUNDS):
                xbuf[r, pl.ds(land, RADIUS)] = jnp.zeros(
                    (RADIUS, tile_y, depth), jnp.float32
                )

    tail_at = {last: RADIUS, last - 1: 2 * RADIUS * even, groups: 2 * RADIUS * odd}

    @pl.when(jnp.logical_not(has_beyond))
    def _():
        tail[pl.ds(tail_at[groups], RADIUS)] = jnp.zeros(
            (RADIUS, tile_y, depth), jnp.float32
        )

    z_taps[...] = depth_matrix(depth)

    peers = jnp.int32(len(others))
    for there, _ in greeted:
        peers = peers + there.astype(jnp.int32)
    pl.semaphore_wait(barrier, peers)

    sent_rows = (RADIUS, tile_y)
    landing = (RADIUS + tile_y, 0)

    def rows_of(r, j, low, n, source):
        part = pl.ds(starts[j], RADIUS)
        if source is None:
            return ubuf.at[r, part, pl.ds(low, n)]
        return source.at[part, pl.ds(low - RADIUS, n)]

    def y_copy(r, d, j, source=None):
        return pltpu.make_async_remote_copy(
            src_ref=rows_of(r, j, sent_rows[d], RADIUS, source),
            dst_ref=ubuf.at[r, pl.ds(starts[j], RADIUS), pl.ds(landing[d], RADIUS)],
            send_sem=y_send.at[r, d, j],
            recv_sem=y_recv.at[r, d, j],
            device_id=y_device[d],
            device_id_type=MESH,
        )

    def corner_copy(r, d, source=None):
        return pltpu.make_async_remote_copy(
            src_ref=rows_of(r, last, sent_rows[d], RADIUS, source),
            dst_ref=ubuf.at[r, pl.ds(tile_x, RADIUS), pl.ds(landing[d], RADIUS)],
            send_sem=t_send.at[r, d],
            recv_sem=t_recv.at[r, d],
            device_id=c_device[d],
            device_id_type=MESH,
        )

    def beyond_copy(r, source=None):
        return pltpu.make_async_remote_copy(
            src_ref=rows_of(r, last, RADIUS, tile_y, source),
            dst_ref=ubuf.at[r, pl.ds(tile_x, RADIUS), own],
            send_sem=t_send.at[r, 2],
            recv_sem=t_recv.at[r, 2],
            device_id={"gx": beyond},
            device_id_type=MESH,
        )

    def pair_copy(r, land):
        return pltpu.make_async_remote_copy(
            src_ref=xbuf.at[r, pl.ds(RADIUS + starts[0], RADIUS)],
            dst_ref=xbuf.at[r, pl.ds(land, RADIUS)],
            send_sem=x_send.at[r],
            recv_sem=x_recv.at[r],
            device_id={"gx": pair},
            device_id_type=MESH,
        )

    def s_copy(k, j, slot):
        part = pl.ds(starts[j], RADIUS)
        return pltpu.make_async_remote_copy(
            src_ref=sens.at[me, part],
            dst_ref=sens.at[slot, part],
            send_sem=s_send.at[k, j],
            recv_sem=s_recv.at[k, j],
            device_id=others[k],
            device_id_type=MESH,
        )

    def send(r, j, source=None):
        if j == last:
            for d in (0, 1):

                @pl.when(c_there[d])
                def _(d=d):
                    corner_copy(r, d, source).start()

        for d in (0, 1):

            @pl.when(y_there[d])
            def _(d=d):
                y_copy(r, d, j, source).start()

        if j == last:

            @pl.when(has_beyond)
            def _():
                beyond_copy(r, source).start()

    for j in (0, 1):
        send(0, j, den)

    for j in range(groups):
        if j == 1:
            for i in (last, *range(2, last)):
                send(0, i, den)
        loads["f", j].wait()
        loads["a", j].wait()
        for i in range(RADIUS):
            q = starts[j] + i
            total = None
            for s in range(sources):
                real = None
                for c in range(comps):
                    a = fbuf[s, 0, c, q].astype(jnp.float32) * abuf[s, 0, c, q].astype(
                        jnp.float32
                    )
                    b = fbuf[s, 1, c, q].astype(jnp.float32) * abuf[s, 1, c, q].astype(
                        jnp.float32
                    )
                    real = (a - b) if real is None else real + (a - b)
                term = weight[s] * real
                total = term if total is None else total + term
            sens[me, q] = total
        if j >= LATE_FROM:

            @pl.when(odd == 0)
            def _(j=j):
                for k in range(len(others)):
                    s_copy(k, j, me).start()

        else:
            for k in range(len(others)):
                s_copy(k, j, me).start()

    def taps(ref, step, n):
        one, two, three, four, five = (
            ref[:, pl.ds(step * k, n)] for k in range(5)
        )
        return (one + five) + 2.0 * (two + four) + 3.0 * three

    def store(r, out, j, total):
        if r == ROUNDS - 1 and j in tail_at:
            tail[pl.ds(tail_at[j], RADIUS)] = total
        if r < ROUNDS - 1 or j <= last:
            xbuf[r, pl.ds(out, RADIUS)] = total

    def filter_rows(r, start, out, j):
        near = pl.ds(0, tile_y + 12)
        stage[:, near] = taps(ubuf.at[r, pl.ds(start, RADIUS)], 1, tile_y + 12)
        total = taps(stage, 3, tile_y)
        store(r, out, j, total)

    def y_filter(r, j):
        for d, there in ((0, y_there[1]), (1, y_there[0])):

            @pl.when(there)
            def _(d=d):
                y_copy(r, d, j).wait_recv()

        filter_rows(r, starts[j], RADIUS + starts[j], j)
        if j == 0:

            @pl.when(has_pair)
            def _():
                pair_copy(r, odd * (tile_x + RADIUS)).start()

    def pair_arrive(r):
        @pl.when(has_pair)
        def _():
            pair_copy(r, pair_land).wait_recv()

    def beyond_filter(r):
        for d in (0, 1):

            @pl.when(c_there[1 - d])
            def _(d=d):
                corner_copy(r, d).wait_recv()

        @pl.when(has_beyond)
        def _():
            beyond_copy(r).wait_recv()
            filter_rows(r, tile_x, beyond_land, groups)

    def xz_filter(r, j):
        return xz_rows(xbuf[r, pl.ds(starts[j], 3 * RADIUS)], z_taps[...])

    def chain(j, filtered):
        part = pl.ds(starts[j], RADIUS)
        for k in range(len(others)):
            s_copy(k, j, lax.rem(me + n_illum - 1 - k, n_illum)).wait_recv()
        total = sens[0, part]
        for e in range(1, n_illum):
            total = total + sens[e, part]
        inner = jnp.tanh(SHARPNESS * (filtered - THRESHOLD))
        ubuf[1, part, own] = total * (SHARPNESS * (1.0 - inner * inner) * (1.0 / SCALE))
        send(1, j)

    def update(j, gradient):
        part = pl.ds(starts[j], RADIUS)
        one = 0.9 * m1buf[part] + 0.1 * gradient
        two = 0.999 * m2buf[part] + 0.001 * gradient * gradient
        step = one * FIRST_FIX / (jnp.sqrt(two * SECOND_FIX) + 1e-08)
        value = jnp.clip(ubuf[0, part, own] - 0.05 * step, 0.0, 1.0)
        ubuf[2, part, own] = value
        send(2, j)
        new_m1[part] = one
        new_m2[part] = two
        new_den[part] = value

    def finish(j, value):
        part = pl.ds(starts[j], RADIUS)
        physical[part] = project(value)

    def drain(r):
        source = den if r == 0 else None
        for d in (0, 1):

            @pl.when(y_there[d])
            def _(d=d):
                for j in range(groups):
                    y_copy(r, d, j, source).wait_send()

            @pl.when(c_there[d])
            def _(d=d):
                corner_copy(r, d, source).wait_send()

        @pl.when(has_beyond)
        def _():
            beyond_copy(r, source).wait_send()

        @pl.when(has_pair)
        def _():
            pair_copy(r, odd * (tile_x + RADIUS)).wait_send()

    def drain_early():
        for j in range(groups):
            for k in range(len(others)):
                s_copy(k, j, me).wait_send()
        for r in range(ROUNDS - 1):
            drain(r)

    loads["d"].wait()
    steps = plan(groups)
    for r, point in enumerate((chain, update, finish)):
        if r == 1:
            loads["m1"].wait()
            loads["m2"].wait()
        for step, j in steps[r]:
            if step == "y":
                y_filter(r, j)
            elif step == "pair":
                pair_arrive(r)
            elif step == "beyond":
                if r == ROUNDS - 1:
                    drain_early()
                beyond_filter(r)
            elif step == "late":

                @pl.when(odd == 1)
                def _(late=(range(1, 3), range(3, groups))[j]):
                    for j in late:
                        for k in range(len(others)):
                            s_copy(k, j, me).start()

            elif r < ROUNDS - 1 or j < last:
                point(j, xz_filter(r, j))

    drain(ROUNDS - 1)


def export(a, b, c, d, tail, z_taps, a_out, b_out, c_out, d_out, edge, sem):
    tile_x = d.shape[0]
    even = 1 - lax.rem(lax.axis_index("gx"), 2)
    done = pl.ds(RADIUS * even, tile_x - RADIUS)
    copies = [
        pltpu.make_async_copy(src, dst, sem.at[i])
        for i, (src, dst) in enumerate(
            ((d.at[done], d_out.at[done]), (a, a_out), (b, b_out), (c, c_out))
        )
    ]
    for copy in copies:
        copy.start()
    edge[...] = project(xz_rows(tail[...], z_taps[...]))
    final = pltpu.make_async_copy(
        edge, d_out.at[pl.ds((tile_x - RADIUS) * (1 - even), RADIUS)], sem.at[4]
    )
    final.start()
    for copy in (*copies, final):
        copy.wait()


def shards(sizes, density, moment_one, moment_two, forward_field, adjoint_field, objective_weight):
    tile_x, tile_y, depth = density.shape
    n_illum = sizes[0]
    tile = jax.ShapeDtypeStruct(density.shape, jnp.float32)
    f32 = jnp.float32
    far = max(n_illum - 1, 1)
    groups = tile_x // RADIUS
    arguments = [
        pltpu.with_memory_space_constraint(x, pltpu.HBM)
        for x in (density, moment_one, moment_two, forward_field, adjoint_field)
    ]
    results = pl.pallas_call(
        functools.partial(kernel, sizes),
        out_shape=(pltpu.VMEM(density.shape, f32),) * 4
        + (
            pltpu.VMEM((3 * RADIUS, tile_y, depth), f32),
            pltpu.VMEM((2 * depth, depth), jnp.bfloat16),
        ),
        in_specs=[pl.BlockSpec(memory_space=pltpu.HBM)] * 5
        + [pl.BlockSpec(memory_space=pltpu.SMEM)],
        out_specs=(pl.BlockSpec(memory_space=pltpu.VMEM),) * 6,
        scratch_shapes=[
            pltpu.VMEM(
                (ROUNDS, tile_x + RADIUS, tile_y + 2 * RADIUS, depth), f32
            ),
            pltpu.VMEM((ROUNDS, tile_x + 2 * RADIUS, tile_y, depth), f32),
            pltpu.VMEM((n_illum, tile_x, tile_y, depth), f32),
            pltpu.VMEM(forward_field.shape, forward_field.dtype),
            pltpu.VMEM(adjoint_field.shape, adjoint_field.dtype),
            pltpu.VMEM(density.shape, f32),
            pltpu.VMEM(density.shape, f32),
            pltpu.VMEM((RADIUS, tile_y + 2 * RADIUS, depth), f32),
            pltpu.SemaphoreType.DMA((2 * groups + 3,)),
            pltpu.SemaphoreType.DMA((ROUNDS, 2, groups)),
            pltpu.SemaphoreType.DMA((ROUNDS, 2, groups)),
            pltpu.SemaphoreType.DMA((ROUNDS, 3)),
            pltpu.SemaphoreType.DMA((ROUNDS, 3)),
            pltpu.SemaphoreType.DMA((ROUNDS,)),
            pltpu.SemaphoreType.DMA((ROUNDS,)),
            pltpu.SemaphoreType.DMA((far, groups)),
            pltpu.SemaphoreType.DMA((far, groups)),
        ],
        compiler_params=pltpu.CompilerParams(
            collective_id=0, has_side_effects=True, vmem_limit_bytes=48 << 20
        ),
        name="design_update",
    )(*arguments, objective_weight)
    return pl.pallas_call(
        export,
        out_shape=(tile,) * 4,
        in_specs=[pl.BlockSpec(memory_space=pltpu.VMEM)] * 6,
        out_specs=(pl.BlockSpec(memory_space=pl.ANY),) * 4,
        scratch_shapes=[
            pltpu.VMEM((RADIUS, tile_y, depth), f32),
            pltpu.SemaphoreType.DMA((5,)),
        ],
        compiler_params=pltpu.CompilerParams(vmem_limit_bytes=4 << 20),
        name="export_results",
    )(*results)


def solution(mesh):
    field = P("illum", None, None, "gx", "gy", None)
    tile = P("gx", "gy", None)
    sizes = (mesh.shape["illum"], mesh.shape["gx"], mesh.shape["gy"])
    return jax.shard_map(
        functools.partial(shards, sizes),
        mesh=mesh,
        in_specs=(tile, tile, tile, field, field, P("illum")),
        out_specs=(tile,) * 4,
        check_vma=False,
    )
```

```python
import functools
import math

import jax
import jax.numpy as jnp
from jax import lax
from jax.experimental import pallas as pl
from jax.experimental.pallas import tpu as pltpu
from jax.sharding import PartitionSpec as P

RADIUS = 8
SHARPNESS = 8.0
THRESHOLD = 0.5
TANH_EDGE = math.tanh(SHARPNESS * THRESHOLD)
SCALE = math.tanh(SHARPNESS * THRESHOLD) + math.tanh(SHARPNESS * (1.0 - THRESHOLD))
NORM = 1.0 / float((RADIUS + 1) ** 6)
FIRST_FIX = 1.0 / (1.0 - 0.9**5)
SECOND_FIX = 1.0 / (1.0 - 0.999**5)
MESH = pl.DeviceIdType.MESH
ROUNDS = 3
LATE_FROM = 1


def plan(groups):
    last = groups - 1
    sweep = [("y", 0), ("y", 1), ("pair", 0), ("out", 0)]
    for j in range(2, groups):
        sweep += [("y", j), ("out", j - 1)]
    first = sweep[:1] + [("late", 0)] + sweep[1:2] + [("late", 1)] + sweep[2:] + [("beyond", 0), ("out", last)]
    second = sweep[:-1] + [("beyond", 0), ("out", last), ("out", last - 1)]
    third = [("y", j) for j in range(groups)]
    third += [("pair", 0), ("out", 0), ("middle", 0), ("beyond", 0)]
    return first, second, third


def split(value):
    high = value.astype(jnp.bfloat16)
    low = (value - high.astype(jnp.float32)).astype(jnp.bfloat16)
    return high, low


def box(value):
    n = value.shape[0]
    two = value[: n - 1] + value[1:]
    four = two[: n - 3] + two[2:]
    eight = four[: n - 7] + four[4:]
    return eight[: n - 8] + value[8:]


def project(value):
    return (TANH_EDGE + jnp.tanh(SHARPNESS * (value - THRESHOLD))) * (1.0 / SCALE)


def xz_rows(value, z_taps):
    n, tile_y, depth = value.shape
    value = box(box(value)).reshape((n - 2 * RADIUS) * tile_y, depth)
    both = jnp.concatenate(split(value), axis=1)
    out = jnp.dot(both, z_taps, preferred_element_type=jnp.float32)
    return (out * NORM).reshape(n - 2 * RADIUS, tile_y, depth)


def depth_matrix(length):
    row = lax.broadcasted_iota(jnp.int32, (2 * length, length), 0)
    col = lax.broadcasted_iota(jnp.int32, (2 * length, length), 1)
    row = jnp.where(row >= length, row - length, row)
    taps = jnp.maximum(RADIUS + 1 - jnp.abs(row - col), 0)
    return taps.astype(jnp.float32).astype(jnp.bfloat16)


def kernel(
    sizes,
    den,
    m1,
    m2,
    fwd,
    adj,
    weight,
    new_den,
    new_m1,
    new_m2,
    physical,
    tail,
    z_taps,
    ubuf,
    xbuf,
    sens,
    fbuf,
    abuf,
    m1buf,
    m2buf,
    stage,
    local_sem,
    y_send,
    y_recv,
    t_send,
    t_recv,
    x_send,
    x_recv,
    s_send,
    s_recv,
):
    n_illum, n_gx, n_gy = sizes
    tile_x, tile_y, depth = den.shape
    sources, _, comps = fwd.shape[:3]
    groups = tile_x // RADIUS
    last = groups - 1
    me = lax.axis_index("illum")
    gx = lax.axis_index("gx")
    gy = lax.axis_index("gy")
    odd = lax.rem(gx, 2)
    even = 1 - odd
    reach = tile_x - RADIUS
    starts = [even * (reach - 2 * RADIUS * j) + RADIUS * j for j in range(groups)]
    own = pl.ds(RADIUS, tile_y)

    pair = gx + even - odd
    beyond = gx - even + odd
    has_pair = jnp.logical_and(pair >= 0, pair < n_gx)
    has_beyond = jnp.logical_and(beyond >= 0, beyond < n_gx)
    pair = jnp.clip(pair, 0, n_gx - 1)
    beyond = jnp.clip(beyond, 0, n_gx - 1)
    y_there = (gy > 0, gy < n_gy - 1)
    y_at = (jnp.maximum(gy - 1, 0), jnp.minimum(gy + 1, n_gy - 1))
    y_device = [{"gy": at} for at in y_at]
    c_there = [jnp.logical_and(has_beyond, there) for there in y_there]
    c_device = [{"gx": beyond, "gy": at} for at in y_at]
    others = [{"illum": lax.rem(me + k, n_illum)} for k in range(1, n_illum)]

    barrier = pltpu.get_barrier_semaphore()
    greeted = [
        (y_there[0], y_device[0]),
        (y_there[1], y_device[1]),
        (has_pair, {"gx": pair}),
        (has_beyond, {"gx": beyond}),
        (c_there[0], c_device[0]),
        (c_there[1], c_device[1]),
    ]
    for device in others:
        pl.semaphore_signal(barrier, inc=1, device_id=device, device_id_type=MESH)

    for there, device in greeted:

        @pl.when(there)
        def _(device=device):
            pl.semaphore_signal(barrier, inc=1, device_id=device, device_id_type=MESH)


    loads = {}

    def load(name, src, dst):
        copy = pltpu.make_async_copy(src, dst, local_sem.at[len(loads)])
        copy.start()
        loads[name] = copy

    for j in range(groups):
        part = pl.ds(starts[j], RADIUS)
        load(("f", j), fwd.at[:, :, :, part], fbuf.at[:, :, :, part])
        load(("a", j), adj.at[:, :, :, part], abuf.at[:, :, :, part])
    load("d", den, ubuf.at[0, pl.ds(0, tile_x), own])
    load("m1", m1, m1buf)
    load("m2", m2, m2buf)

    for there, land in ((y_there[0], 0), (y_there[1], RADIUS + tile_y)):

        @pl.when(jnp.logical_not(there))
        def _(land=land):
            for r in range(ROUNDS):
                ubuf[r, :, pl.ds(land, RADIUS)] = jnp.zeros(
                    (tile_x + RADIUS, RADIUS, depth), jnp.float32
                )

    pair_land = even * (tile_x + RADIUS)
    beyond_land = odd * (tile_x + RADIUS)
    for there, land in ((has_pair, pair_land), (has_beyond, beyond_land)):

        @pl.when(jnp.logical_not(there))
        def _(land=land):
            for r in range(ROUNDS):
                xbuf[r, pl.ds(land, RADIUS)] = jnp.zeros(
                    (RADIUS, tile_y, depth), jnp.float32
                )

    tail_at = {last: RADIUS, last - 1: 2 * RADIUS * even, groups: 2 * RADIUS * odd}

    @pl.when(jnp.logical_not(has_beyond))
    def _():
        tail[pl.ds(tail_at[groups], RADIUS)] = jnp.zeros(
            (RADIUS, tile_y, depth), jnp.float32
        )

    z_taps[...] = depth_matrix(depth)

    peers = jnp.int32(len(others))
    for there, _ in greeted:
        peers = peers + there.astype(jnp.int32)
    pl.semaphore_wait(barrier, peers)

    sent_rows = (RADIUS, tile_y)
    landing = (RADIUS + tile_y, 0)

    def rows_of(r, j, low, n, source):
        part = pl.ds(starts[j], RADIUS)
        if source is None:
            return ubuf.at[r, part, pl.ds(low, n)]
        return source.at[part, pl.ds(low - RADIUS, n)]

    def y_copy(r, d, j, source=None):
        return pltpu.make_async_remote_copy(
            src_ref=rows_of(r, j, sent_rows[d], RADIUS, source),
            dst_ref=ubuf.at[r, pl.ds(starts[j], RADIUS), pl.ds(landing[d], RADIUS)],
            send_sem=y_send.at[r, d, j],
            recv_sem=y_recv.at[r, d, j],
            device_id=y_device[d],
            device_id_type=MESH,
        )

    def corner_copy(r, d, source=None):
        return pltpu.make_async_remote_copy(
            src_ref=rows_of(r, last, sent_rows[d], RADIUS, source),
            dst_ref=ubuf.at[r, pl.ds(tile_x, RADIUS), pl.ds(landing[d], RADIUS)],
            send_sem=t_send.at[r, d],
            recv_sem=t_recv.at[r, d],
            device_id=c_device[d],
            device_id_type=MESH,
        )

    def beyond_copy(r, source=None):
        return pltpu.make_async_remote_copy(
            src_ref=rows_of(r, last, RADIUS, tile_y, source),
            dst_ref=ubuf.at[r, pl.ds(tile_x, RADIUS), own],
            send_sem=t_send.at[r, 2],
            recv_sem=t_recv.at[r, 2],
            device_id={"gx": beyond},
            device_id_type=MESH,
        )

    def pair_copy(r, land):
        return pltpu.make_async_remote_copy(
            src_ref=xbuf.at[r, pl.ds(RADIUS + starts[0], RADIUS)],
            dst_ref=xbuf.at[r, pl.ds(land, RADIUS)],
            send_sem=x_send.at[r],
            recv_sem=x_recv.at[r],
            device_id={"gx": pair},
            device_id_type=MESH,
        )

    def s_copy(k, j, slot):
        part = pl.ds(starts[j], RADIUS)
        return pltpu.make_async_remote_copy(
            src_ref=sens.at[me, part],
            dst_ref=sens.at[slot, part],
            send_sem=s_send.at[k, j],
            recv_sem=s_recv.at[k, j],
            device_id=others[k],
            device_id_type=MESH,
        )

    def send(r, j, source=None):
        if j == last:
            for d in (0, 1):

                @pl.when(c_there[d])
                def _(d=d):
                    corner_copy(r, d, source).start()

        for d in (0, 1):

            @pl.when(y_there[d])
            def _(d=d):
                y_copy(r, d, j, source).start()

        if j == last:

            @pl.when(has_beyond)
            def _():
                beyond_copy(r, source).start()

    for j in (0, 1):
        send(0, j, den)

    for j in range(groups):
        if j == 1:
            for i in (last, *range(2, last)):
                send(0, i, den)
        loads["f", j].wait()
        loads["a", j].wait()
        for i in range(RADIUS):
            q = starts[j] + i
            total = None
            for s in range(sources):
                real = None
                for c in range(comps):
                    a = fbuf[s, 0, c, q].astype(jnp.float32) * abuf[s, 0, c, q].astype(
                        jnp.float32
                    )
                    b = fbuf[s, 1, c, q].astype(jnp.float32) * abuf[s, 1, c, q].astype(
                        jnp.float32
                    )
                    real = (a - b) if real is None else real + (a - b)
                term = weight[s] * real
                total = term if total is None else total + term
            sens[me, q] = total
        if j >= LATE_FROM:

            @pl.when(odd == 0)
            def _(j=j):
                for k in range(len(others)):
                    s_copy(k, j, me).start()

        else:
            for k in range(len(others)):
                s_copy(k, j, me).start()

    def taps(ref, step, n):
        one, two, three, four, five = (
            ref[:, pl.ds(step * k, n)] for k in range(5)
        )
        return (one + five) + 2.0 * (two + four) + 3.0 * three

    def store(r, out, j, total):
        if r == ROUNDS - 1 and j in tail_at:
            tail[pl.ds(tail_at[j], RADIUS)] = total
        if r < ROUNDS - 1 or j <= last:
            xbuf[r, pl.ds(out, RADIUS)] = total

    def filter_rows(r, start, out, j):
        near = pl.ds(0, tile_y + 12)
        stage[:, near] = taps(ubuf.at[r, pl.ds(start, RADIUS)], 1, tile_y + 12)
        total = taps(stage, 3, tile_y)
        store(r, out, j, total)

    def y_filter(r, j):
        for d, there in ((0, y_there[1]), (1, y_there[0])):

            @pl.when(there)
            def _(d=d):
                y_copy(r, d, j).wait_recv()

        filter_rows(r, starts[j], RADIUS + starts[j], j)
        if j == 0:

            @pl.when(has_pair)
            def _():
                pair_copy(r, odd * (tile_x + RADIUS)).start()

    def pair_arrive(r):
        @pl.when(has_pair)
        def _():
            pair_copy(r, pair_land).wait_recv()

    def beyond_filter(r):
        for d in (0, 1):

            @pl.when(c_there[1 - d])
            def _(d=d):
                corner_copy(r, d).wait_recv()

        @pl.when(has_beyond)
        def _():
            beyond_copy(r).wait_recv()
            filter_rows(r, tile_x, beyond_land, groups)

    def xz_filter(r, j):
        return xz_rows(xbuf[r, pl.ds(starts[j], 3 * RADIUS)], z_taps[...])

    def chain(j, filtered):
        part = pl.ds(starts[j], RADIUS)
        for k in range(len(others)):
            s_copy(k, j, lax.rem(me + n_illum - 1 - k, n_illum)).wait_recv()
        total = sens[0, part]
        for e in range(1, n_illum):
            total = total + sens[e, part]
        inner = jnp.tanh(SHARPNESS * (filtered - THRESHOLD))
        ubuf[1, part, own] = total * (SHARPNESS * (1.0 - inner * inner) * (1.0 / SCALE))
        send(1, j)

    def update(j, gradient):
        part = pl.ds(starts[j], RADIUS)
        one = 0.9 * m1buf[part] + 0.1 * gradient
        two = 0.999 * m2buf[part] + 0.001 * gradient * gradient
        step = one * FIRST_FIX / (jnp.sqrt(two * SECOND_FIX) + 1e-08)
        value = jnp.clip(ubuf[0, part, own] - 0.05 * step, 0.0, 1.0)
        ubuf[2, part, own] = value
        send(2, j)
        new_m1[part] = one
        new_m2[part] = two
        new_den[part] = value

    def finish(j, value):
        part = pl.ds(starts[j], RADIUS)
        physical[part] = project(value)

    def drain(r):
        source = den if r == 0 else None
        for d in (0, 1):

            @pl.when(y_there[d])
            def _(d=d):
                for j in range(groups):
                    y_copy(r, d, j, source).wait_send()

            @pl.when(c_there[d])
            def _(d=d):
                corner_copy(r, d, source).wait_send()

        @pl.when(has_beyond)
        def _():
            beyond_copy(r, source).wait_send()

        @pl.when(has_pair)
        def _():
            pair_copy(r, odd * (tile_x + RADIUS)).wait_send()

    def drain_early():
        for j in range(groups):
            for k in range(len(others)):
                s_copy(k, j, me).wait_send()
        for r in range(ROUNDS - 1):
            drain(r)

    loads["d"].wait()
    steps = plan(groups)
    for r, point in enumerate((chain, update, finish)):
        if r == 1:
            loads["m1"].wait()
            loads["m2"].wait()
        for step, j in steps[r]:
            if step == "y":
                y_filter(r, j)
            elif step == "pair":
                pair_arrive(r)
            elif step == "beyond":
                if r == ROUNDS - 1:
                    drain_early()
                beyond_filter(r)
            elif step == "late":

                @pl.when(odd == 1)
                def _(late=(range(1, 3), range(3, groups))[j]):
                    for j in late:
                        for k in range(len(others)):
                            s_copy(k, j, me).start()

            elif step == "middle":
                inner = xbuf[r, pl.ds(RADIUS, tile_x)]
                physical[pl.ds(RADIUS, tile_x - 2 * RADIUS)] = project(
                    xz_rows(inner, z_taps[...])
                )
            elif r < ROUNDS - 1 or j < last:
                point(j, xz_filter(r, j))

    drain(ROUNDS - 1)


def export(a, b, c, d, tail, z_taps, a_out, b_out, c_out, d_out, edge, sem):
    tile_x = d.shape[0]
    even = 1 - lax.rem(lax.axis_index("gx"), 2)
    done = pl.ds(RADIUS * even, tile_x - RADIUS)
    copies = [
        pltpu.make_async_copy(src, dst, sem.at[i])
        for i, (src, dst) in enumerate(
            ((d.at[done], d_out.at[done]), (a, a_out), (b, b_out), (c, c_out))
        )
    ]
    for copy in copies:
        copy.start()
    edge[...] = project(xz_rows(tail[...], z_taps[...]))
    final = pltpu.make_async_copy(
        edge, d_out.at[pl.ds((tile_x - RADIUS) * (1 - even), RADIUS)], sem.at[4]
    )
    final.start()
    for copy in (*copies, final):
        copy.wait()


def shards(sizes, density, moment_one, moment_two, forward_field, adjoint_field, objective_weight):
    tile_x, tile_y, depth = density.shape
    n_illum = sizes[0]
    tile = jax.ShapeDtypeStruct(density.shape, jnp.float32)
    f32 = jnp.float32
    far = max(n_illum - 1, 1)
    groups = tile_x // RADIUS
    arguments = [
        pltpu.with_memory_space_constraint(x, pltpu.HBM)
        for x in (density, moment_one, moment_two, forward_field, adjoint_field)
    ]
    results = pl.pallas_call(
        functools.partial(kernel, sizes),
        out_shape=(pltpu.VMEM(density.shape, f32),) * 4
        + (
            pltpu.VMEM((3 * RADIUS, tile_y, depth), f32),
            pltpu.VMEM((2 * depth, depth), jnp.bfloat16),
        ),
        in_specs=[pl.BlockSpec(memory_space=pltpu.HBM)] * 5
        + [pl.BlockSpec(memory_space=pltpu.SMEM)],
        out_specs=(pl.BlockSpec(memory_space=pltpu.VMEM),) * 6,
        scratch_shapes=[
            pltpu.VMEM(
                (ROUNDS, tile_x + RADIUS, tile_y + 2 * RADIUS, depth), f32
            ),
            pltpu.VMEM((ROUNDS, tile_x + 2 * RADIUS, tile_y, depth), f32),
            pltpu.VMEM((n_illum, tile_x, tile_y, depth), f32),
            pltpu.VMEM(forward_field.shape, forward_field.dtype),
            pltpu.VMEM(adjoint_field.shape, adjoint_field.dtype),
            pltpu.VMEM(density.shape, f32),
            pltpu.VMEM(density.shape, f32),
            pltpu.VMEM((RADIUS, tile_y + 2 * RADIUS, depth), f32),
            pltpu.SemaphoreType.DMA((2 * groups + 3,)),
            pltpu.SemaphoreType.DMA((ROUNDS, 2, groups)),
            pltpu.SemaphoreType.DMA((ROUNDS, 2, groups)),
            pltpu.SemaphoreType.DMA((ROUNDS, 3)),
            pltpu.SemaphoreType.DMA((ROUNDS, 3)),
            pltpu.SemaphoreType.DMA((ROUNDS,)),
            pltpu.SemaphoreType.DMA((ROUNDS,)),
            pltpu.SemaphoreType.DMA((far, groups)),
            pltpu.SemaphoreType.DMA((far, groups)),
        ],
        compiler_params=pltpu.CompilerParams(
            collective_id=0, has_side_effects=True, vmem_limit_bytes=48 << 20
        ),
        name="design_update",
    )(*arguments, objective_weight)
    return pl.pallas_call(
        export,
        out_shape=(tile,) * 4,
        in_specs=[pl.BlockSpec(memory_space=pltpu.VMEM)] * 6,
        out_specs=(pl.BlockSpec(memory_space=pl.ANY),) * 4,
        scratch_shapes=[
            pltpu.VMEM((RADIUS, tile_y, depth), f32),
            pltpu.SemaphoreType.DMA((5,)),
        ],
        compiler_params=pltpu.CompilerParams(vmem_limit_bytes=4 << 20),
        name="export_results",
    )(*results)


def solution(mesh):
    field = P("illum", None, None, "gx", "gy", None)
    tile = P("gx", "gy", None)
    sizes = (mesh.shape["illum"], mesh.shape["gx"], mesh.shape["gy"])
    return jax.shard_map(
        functools.partial(shards, sizes),
        mesh=mesh,
        in_specs=(tile, tile, tile, field, field, P("illum")),
        out_specs=(tile,) * 4,
        check_vma=False,
    )
```

```python
import functools
import math

import jax
import jax.numpy as jnp
from jax import lax
from jax.experimental import pallas as pl
from jax.experimental.pallas import tpu as pltpu
from jax.sharding import PartitionSpec as P

RADIUS = 8
SHARPNESS = 8.0
THRESHOLD = 0.5
TANH_EDGE = math.tanh(SHARPNESS * THRESHOLD)
SCALE = math.tanh(SHARPNESS * THRESHOLD) + math.tanh(SHARPNESS * (1.0 - THRESHOLD))
NORM = 1.0 / float((RADIUS + 1) ** 6)
FIRST_FIX = 1.0 / (1.0 - 0.9**5)
SECOND_FIX = 1.0 / (1.0 - 0.999**5)
MESH = pl.DeviceIdType.MESH
ROUNDS = 3
LATE_FROM = 1


def plan(groups):
    last = groups - 1
    sweep = [("y", 0), ("y", 1), ("pair", 0), ("out", 0)]
    for j in range(2, groups):
        sweep += [("y", j), ("out", j - 1)]
    first = sweep[:1] + [("late", 0)] + sweep[1:2] + [("late", 1)] + sweep[2:-1]
    first += [("beyond", 0), ("out", last - 1), ("out", last)]
    second = sweep[:-1] + [("beyond", 0), ("out", last), ("out", last - 1)]
    third = [("y", j) for j in range(groups)]
    third += [("pair", 0), ("near", 0), ("beyond", 0)]
    return first, second, third


def split(value):
    high = value.astype(jnp.bfloat16)
    low = (value - high.astype(jnp.float32)).astype(jnp.bfloat16)
    return high, low


def box(value):
    n = value.shape[0]
    two = value[: n - 1] + value[1:]
    four = two[: n - 3] + two[2:]
    eight = four[: n - 7] + four[4:]
    return eight[: n - 8] + value[8:]


def project(value):
    return (TANH_EDGE + jnp.tanh(SHARPNESS * (value - THRESHOLD))) * (1.0 / SCALE)


def xz_rows(value, z_taps):
    n, tile_y, depth = value.shape
    value = box(box(value)).reshape((n - 2 * RADIUS) * tile_y, depth)
    both = jnp.concatenate(split(value), axis=1)
    out = jnp.dot(both, z_taps, preferred_element_type=jnp.float32)
    return (out * NORM).reshape(n - 2 * RADIUS, tile_y, depth)


def depth_matrix(length):
    row = lax.broadcasted_iota(jnp.int32, (2 * length, length), 0)
    col = lax.broadcasted_iota(jnp.int32, (2 * length, length), 1)
    row = jnp.where(row >= length, row - length, row)
    taps = jnp.maximum(RADIUS + 1 - jnp.abs(row - col), 0)
    return taps.astype(jnp.float32).astype(jnp.bfloat16)


def kernel(
    sizes,
    den,
    m1,
    m2,
    fwd,
    adj,
    weight,
    new_den,
    new_m1,
    new_m2,
    physical,
    tail,
    z_taps,
    ubuf,
    xbuf,
    sens,
    fbuf,
    abuf,
    m1buf,
    m2buf,
    stage,
    local_sem,
    y_send,
    y_recv,
    t_send,
    t_recv,
    x_send,
    x_recv,
    s_send,
    s_recv,
):
    n_illum, n_gx, n_gy = sizes
    tile_x, tile_y, depth = den.shape
    sources, _, comps = fwd.shape[:3]
    groups = tile_x // RADIUS
    last = groups - 1
    me = lax.axis_index("illum")
    gx = lax.axis_index("gx")
    gy = lax.axis_index("gy")
    odd = lax.rem(gx, 2)
    even = 1 - odd
    reach = tile_x - RADIUS
    starts = [even * (reach - 2 * RADIUS * j) + RADIUS * j for j in range(groups)]
    own = pl.ds(RADIUS, tile_y)

    pair = gx + even - odd
    beyond = gx - even + odd
    has_pair = jnp.logical_and(pair >= 0, pair < n_gx)
    has_beyond = jnp.logical_and(beyond >= 0, beyond < n_gx)
    pair = jnp.clip(pair, 0, n_gx - 1)
    beyond = jnp.clip(beyond, 0, n_gx - 1)
    y_there = (gy > 0, gy < n_gy - 1)
    y_at = (jnp.maximum(gy - 1, 0), jnp.minimum(gy + 1, n_gy - 1))
    y_device = [{"gy": at} for at in y_at]
    c_there = [jnp.logical_and(has_beyond, there) for there in y_there]
    c_device = [{"gx": beyond, "gy": at} for at in y_at]
    others = [{"illum": lax.rem(me + k, n_illum)} for k in range(1, n_illum)]

    barrier = pltpu.get_barrier_semaphore()
    greeted = [
        (y_there[0], y_device[0]),
        (y_there[1], y_device[1]),
        (has_pair, {"gx": pair}),
        (has_beyond, {"gx": beyond}),
        (c_there[0], c_device[0]),
        (c_there[1], c_device[1]),
    ]
    for device in others:
        pl.semaphore_signal(barrier, inc=1, device_id=device, device_id_type=MESH)

    for there, device in greeted:

        @pl.when(there)
        def _(device=device):
            pl.semaphore_signal(barrier, inc=1, device_id=device, device_id_type=MESH)


    loads = {}

    def load(name, src, dst):
        copy = pltpu.make_async_copy(src, dst, local_sem.at[len(loads)])
        copy.start()
        loads[name] = copy

    for j in range(groups):
        part = pl.ds(starts[j], RADIUS)
        load(("f", j), fwd.at[:, :, :, part], fbuf.at[:, :, :, part])
        load(("a", j), adj.at[:, :, :, part], abuf.at[:, :, :, part])
    load("d", den, ubuf.at[0, pl.ds(0, tile_x), own])
    load("m1", m1, m1buf)
    load("m2", m2, m2buf)

    for there, land in ((y_there[0], 0), (y_there[1], RADIUS + tile_y)):

        @pl.when(jnp.logical_not(there))
        def _(land=land):
            for r in range(ROUNDS):
                ubuf[r, :, pl.ds(land, RADIUS)] = jnp.zeros(
                    (tile_x + RADIUS, RADIUS, depth), jnp.float32
                )

    pair_land = even * (tile_x + RADIUS)
    beyond_land = odd * (tile_x + RADIUS)
    for there, land in ((has_pair, pair_land), (has_beyond, beyond_land)):

        @pl.when(jnp.logical_not(there))
        def _(land=land):
            for r in range(ROUNDS):
                xbuf[r, pl.ds(land, RADIUS)] = jnp.zeros(
                    (RADIUS, tile_y, depth), jnp.float32
                )

    tail_at = {last: RADIUS, last - 1: 2 * RADIUS * even, groups: 2 * RADIUS * odd}

    @pl.when(jnp.logical_not(has_beyond))
    def _():
        tail[pl.ds(tail_at[groups], RADIUS)] = jnp.zeros(
            (RADIUS, tile_y, depth), jnp.float32
        )

    z_taps[...] = depth_matrix(depth)

    peers = jnp.int32(len(others))
    for there, _ in greeted:
        peers = peers + there.astype(jnp.int32)
    pl.semaphore_wait(barrier, peers)

    sent_rows = (RADIUS, tile_y)
    landing = (RADIUS + tile_y, 0)

    def rows_of(r, j, low, n, source):
        part = pl.ds(starts[j], RADIUS)
        if source is None:
            return ubuf.at[r, part, pl.ds(low, n)]
        return source.at[part, pl.ds(low - RADIUS, n)]

    def y_copy(r, d, j, source=None):
        return pltpu.make_async_remote_copy(
            src_ref=rows_of(r, j, sent_rows[d], RADIUS, source),
            dst_ref=ubuf.at[r, pl.ds(starts[j], RADIUS), pl.ds(landing[d], RADIUS)],
            send_sem=y_send.at[r, d, j],
            recv_sem=y_recv.at[r, d, j],
            device_id=y_device[d],
            device_id_type=MESH,
        )

    def corner_copy(r, d, source=None):
        return pltpu.make_async_remote_copy(
            src_ref=rows_of(r, last, sent_rows[d], RADIUS, source),
            dst_ref=ubuf.at[r, pl.ds(tile_x, RADIUS), pl.ds(landing[d], RADIUS)],
            send_sem=t_send.at[r, d],
            recv_sem=t_recv.at[r, d],
            device_id=c_device[d],
            device_id_type=MESH,
        )

    def beyond_copy(r, source=None):
        return pltpu.make_async_remote_copy(
            src_ref=rows_of(r, last, RADIUS, tile_y, source),
            dst_ref=ubuf.at[r, pl.ds(tile_x, RADIUS), own],
            send_sem=t_send.at[r, 2],
            recv_sem=t_recv.at[r, 2],
            device_id={"gx": beyond},
            device_id_type=MESH,
        )

    def pair_copy(r, land):
        return pltpu.make_async_remote_copy(
            src_ref=xbuf.at[r, pl.ds(RADIUS + starts[0], RADIUS)],
            dst_ref=xbuf.at[r, pl.ds(land, RADIUS)],
            send_sem=x_send.at[r],
            recv_sem=x_recv.at[r],
            device_id={"gx": pair},
            device_id_type=MESH,
        )

    def s_copy(k, j, slot):
        part = pl.ds(starts[j], RADIUS)
        return pltpu.make_async_remote_copy(
            src_ref=sens.at[me, part],
            dst_ref=sens.at[slot, part],
            send_sem=s_send.at[k, j],
            recv_sem=s_recv.at[k, j],
            device_id=others[k],
            device_id_type=MESH,
        )

    def send(r, j, source=None):
        if j == last:
            for d in (0, 1):

                @pl.when(c_there[d])
                def _(d=d):
                    corner_copy(r, d, source).start()

        for d in (0, 1):

            @pl.when(y_there[d])
            def _(d=d):
                y_copy(r, d, j, source).start()

        if j == last:

            @pl.when(has_beyond)
            def _():
                beyond_copy(r, source).start()

    for j in (0, 1):
        send(0, j, den)

    for j in range(groups):
        if j == 1:
            for i in (last, *range(2, last)):
                send(0, i, den)
        loads["f", j].wait()
        loads["a", j].wait()
        for i in range(RADIUS):
            q = starts[j] + i
            total = None
            for s in range(sources):
                real = None
                for c in range(comps):
                    a = fbuf[s, 0, c, q].astype(jnp.float32) * abuf[s, 0, c, q].astype(
                        jnp.float32
                    )
                    b = fbuf[s, 1, c, q].astype(jnp.float32) * abuf[s, 1, c, q].astype(
                        jnp.float32
                    )
                    real = (a - b) if real is None else real + (a - b)
                term = weight[s] * real
                total = term if total is None else total + term
            sens[me, q] = total
        if j >= LATE_FROM:

            @pl.when(odd == 0)
            def _(j=j):
                for k in range(len(others)):
                    s_copy(k, j, me).start()

        else:
            for k in range(len(others)):
                s_copy(k, j, me).start()

    def taps(ref, step, n):
        one, two, three, four, five = (
            ref[:, pl.ds(step * k, n)] for k in range(5)
        )
        return (one + five) + 2.0 * (two + four) + 3.0 * three

    def store(r, out, j, total):
        if r == ROUNDS - 1 and j in tail_at:
            tail[pl.ds(tail_at[j], RADIUS)] = total
        if r < ROUNDS - 1 or j <= last:
            xbuf[r, pl.ds(out, RADIUS)] = total

    def filter_rows(r, start, out, j):
        near = pl.ds(0, tile_y + 12)
        stage[:, near] = taps(ubuf.at[r, pl.ds(start, RADIUS)], 1, tile_y + 12)
        total = taps(stage, 3, tile_y)
        store(r, out, j, total)

    def y_filter(r, j):
        for d, there in ((0, y_there[1]), (1, y_there[0])):

            @pl.when(there)
            def _(d=d):
                y_copy(r, d, j).wait_recv()

        filter_rows(r, starts[j], RADIUS + starts[j], j)
        if j == 0:

            @pl.when(has_pair)
            def _():
                pair_copy(r, odd * (tile_x + RADIUS)).start()

    def pair_arrive(r):
        @pl.when(has_pair)
        def _():
            pair_copy(r, pair_land).wait_recv()

    def beyond_filter(r):
        for d in (0, 1):

            @pl.when(c_there[1 - d])
            def _(d=d):
                corner_copy(r, d).wait_recv()

        @pl.when(has_beyond)
        def _():
            beyond_copy(r).wait_recv()
            filter_rows(r, tile_x, beyond_land, groups)

    def xz_filter(r, j):
        return xz_rows(xbuf[r, pl.ds(starts[j], 3 * RADIUS)], z_taps[...])

    def chain(j, filtered):
        part = pl.ds(starts[j], RADIUS)
        for k in range(len(others)):
            s_copy(k, j, lax.rem(me + n_illum - 1 - k, n_illum)).wait_recv()
        total = sens[0, part]
        for e in range(1, n_illum):
            total = total + sens[e, part]
        inner = jnp.tanh(SHARPNESS * (filtered - THRESHOLD))
        ubuf[1, part, own] = total * (SHARPNESS * (1.0 - inner * inner) * (1.0 / SCALE))
        send(1, j)

    def update(j, gradient):
        part = pl.ds(starts[j], RADIUS)
        one = 0.9 * m1buf[part] + 0.1 * gradient
        two = 0.999 * m2buf[part] + 0.001 * gradient * gradient
        step = one * FIRST_FIX / (jnp.sqrt(two * SECOND_FIX) + 1e-08)
        value = jnp.clip(ubuf[0, part, own] - 0.05 * step, 0.0, 1.0)
        ubuf[2, part, own] = value
        send(2, j)
        new_m1[part] = one
        new_m2[part] = two
        new_den[part] = value

    def finish(j, value):
        part = pl.ds(starts[j], RADIUS)
        physical[part] = project(value)

    def drain(r):
        source = den if r == 0 else None
        for d in (0, 1):

            @pl.when(y_there[d])
            def _(d=d):
                for j in range(groups):
                    y_copy(r, d, j, source).wait_send()

            @pl.when(c_there[d])
            def _(d=d):
                corner_copy(r, d, source).wait_send()

        @pl.when(has_beyond)
        def _():
            beyond_copy(r, source).wait_send()

        @pl.when(has_pair)
        def _():
            pair_copy(r, odd * (tile_x + RADIUS)).wait_send()

    def drain_early():
        for j in range(groups):
            for k in range(len(others)):
                s_copy(k, j, me).wait_send()
        for r in range(ROUNDS - 1):
            drain(r)

    loads["d"].wait()
    steps = plan(groups)
    for r, point in enumerate((chain, update, finish)):
        if r == 1:
            loads["m1"].wait()
            loads["m2"].wait()
        for step, j in steps[r]:
            if step == "y":
                y_filter(r, j)
            elif step == "pair":
                pair_arrive(r)
            elif step == "beyond":
                if r == ROUNDS - 1:
                    drain_early()
                beyond_filter(r)
            elif step == "late":

                @pl.when(odd == 1)
                def _(late=(range(1, 3), range(3, groups))[j]):
                    for j in late:
                        for k in range(len(others)):
                            s_copy(k, j, me).start()

            elif step == "near":
                low = RADIUS * even
                near = xbuf[r, pl.ds(low, tile_x + RADIUS)]
                physical[pl.ds(low, tile_x - RADIUS)] = project(
                    xz_rows(near, z_taps[...])
                )
            elif r < ROUNDS - 1 or j < last:
                point(j, xz_filter(r, j))

    drain(ROUNDS - 1)


def export(a, b, c, d, tail, z_taps, a_out, b_out, c_out, d_out, edge, sem):
    tile_x = d.shape[0]
    even = 1 - lax.rem(lax.axis_index("gx"), 2)
    done = pl.ds(RADIUS * even, tile_x - RADIUS)
    copies = [
        pltpu.make_async_copy(src, dst, sem.at[i])
        for i, (src, dst) in enumerate(
            ((d.at[done], d_out.at[done]), (a, a_out), (b, b_out), (c, c_out))
        )
    ]
    for copy in copies:
        copy.start()
    edge[...] = project(xz_rows(tail[...], z_taps[...]))
    final = pltpu.make_async_copy(
        edge, d_out.at[pl.ds((tile_x - RADIUS) * (1 - even), RADIUS)], sem.at[4]
    )
    final.start()
    for copy in (*copies, final):
        copy.wait()


def shards(sizes, density, moment_one, moment_two, forward_field, adjoint_field, objective_weight):
    tile_x, tile_y, depth = density.shape
    n_illum = sizes[0]
    tile = jax.ShapeDtypeStruct(density.shape, jnp.float32)
    f32 = jnp.float32
    far = max(n_illum - 1, 1)
    groups = tile_x // RADIUS
    arguments = [
        pltpu.with_memory_space_constraint(x, pltpu.HBM)
        for x in (density, moment_one, moment_two, forward_field, adjoint_field)
    ]
    results = pl.pallas_call(
        functools.partial(kernel, sizes),
        out_shape=(pltpu.VMEM(density.shape, f32),) * 4
        + (
            pltpu.VMEM((3 * RADIUS, tile_y, depth), f32),
            pltpu.VMEM((2 * depth, depth), jnp.bfloat16),
        ),
        in_specs=[pl.BlockSpec(memory_space=pltpu.HBM)] * 5
        + [pl.BlockSpec(memory_space=pltpu.SMEM)],
        out_specs=(pl.BlockSpec(memory_space=pltpu.VMEM),) * 6,
        scratch_shapes=[
            pltpu.VMEM(
                (ROUNDS, tile_x + RADIUS, tile_y + 2 * RADIUS, depth), f32
            ),
            pltpu.VMEM((ROUNDS, tile_x + 2 * RADIUS, tile_y, depth), f32),
            pltpu.VMEM((n_illum, tile_x, tile_y, depth), f32),
            pltpu.VMEM(forward_field.shape, forward_field.dtype),
            pltpu.VMEM(adjoint_field.shape, adjoint_field.dtype),
            pltpu.VMEM(density.shape, f32),
            pltpu.VMEM(density.shape, f32),
            pltpu.VMEM((RADIUS, tile_y + 2 * RADIUS, depth), f32),
            pltpu.SemaphoreType.DMA((2 * groups + 3,)),
            pltpu.SemaphoreType.DMA((ROUNDS, 2, groups)),
            pltpu.SemaphoreType.DMA((ROUNDS, 2, groups)),
            pltpu.SemaphoreType.DMA((ROUNDS, 3)),
            pltpu.SemaphoreType.DMA((ROUNDS, 3)),
            pltpu.SemaphoreType.DMA((ROUNDS,)),
            pltpu.SemaphoreType.DMA((ROUNDS,)),
            pltpu.SemaphoreType.DMA((far, groups)),
            pltpu.SemaphoreType.DMA((far, groups)),
        ],
        compiler_params=pltpu.CompilerParams(
            collective_id=0, has_side_effects=True, vmem_limit_bytes=48 << 20
        ),
        name="design_update",
    )(*arguments, objective_weight)
    return pl.pallas_call(
        export,
        out_shape=(tile,) * 4,
        in_specs=[pl.BlockSpec(memory_space=pltpu.VMEM)] * 6,
        out_specs=(pl.BlockSpec(memory_space=pl.ANY),) * 4,
        scratch_shapes=[
            pltpu.VMEM((RADIUS, tile_y, depth), f32),
            pltpu.SemaphoreType.DMA((5,)),
        ],
        compiler_params=pltpu.CompilerParams(vmem_limit_bytes=4 << 20),
        name="export_results",
    )(*results)


def solution(mesh):
    field = P("illum", None, None, "gx", "gy", None)
    tile = P("gx", "gy", None)
    sizes = (mesh.shape["illum"], mesh.shape["gx"], mesh.shape["gy"])
    return jax.shard_map(
        functools.partial(shards, sizes),
        mesh=mesh,
        in_specs=(tile, tile, tile, field, field, P("illum")),
        out_specs=(tile,) * 4,
        check_vma=False,
    )
```

```python
import functools
import math

import jax
import jax.numpy as jnp
from jax import lax
from jax.experimental import pallas as pl
from jax.experimental.pallas import tpu as pltpu
from jax.sharding import PartitionSpec as P

RADIUS = 8
SHARPNESS = 8.0
THRESHOLD = 0.5
TANH_EDGE = math.tanh(SHARPNESS * THRESHOLD)
SCALE = math.tanh(SHARPNESS * THRESHOLD) + math.tanh(SHARPNESS * (1.0 - THRESHOLD))
NORM = 1.0 / float((RADIUS + 1) ** 6)
FIRST_FIX = 1.0 / (1.0 - 0.9**5)
SECOND_FIX = 1.0 / (1.0 - 0.999**5)
MESH = pl.DeviceIdType.MESH
ROUNDS = 3
LATE_FROM = 1


def plan(groups):
    last = groups - 1
    sweep = [("y", 0), ("y", 1), ("pair", 0), ("out", 0)]
    for j in range(2, groups):
        sweep += [("y", j), ("out", j - 1)]
    first = sweep[:1] + [("late", 0)] + sweep[1:2] + [("late", 1)] + sweep[2:] + [("beyond", 0), ("out", last)]
    second = sweep[:-1] + [("beyond", 0), ("out", last), ("out", last - 1)]
    third = [("y", j) for j in range(groups)]
    third += [("pair", 0), ("out", 0), ("middle", 0), ("beyond", 0)]
    return first, second, third


def split(value):
    high = value.astype(jnp.bfloat16)
    low = (value - high.astype(jnp.float32)).astype(jnp.bfloat16)
    return high, low


def box(value):
    n = value.shape[0]
    two = value[: n - 1] + value[1:]
    four = two[: n - 3] + two[2:]
    eight = four[: n - 7] + four[4:]
    return eight[: n - 8] + value[8:]


def project(value):
    return (TANH_EDGE + jnp.tanh(SHARPNESS * (value - THRESHOLD))) * (1.0 / SCALE)


def xz_rows(value, z_taps):
    n, tile_y, depth = value.shape
    value = box(box(value)).reshape((n - 2 * RADIUS) * tile_y, depth)
    both = jnp.concatenate(split(value), axis=1)
    out = jnp.dot(both, z_taps, preferred_element_type=jnp.float32)
    return (out * NORM).reshape(n - 2 * RADIUS, tile_y, depth)


def depth_matrix(length):
    row = lax.broadcasted_iota(jnp.int32, (2 * length, length), 0)
    col = lax.broadcasted_iota(jnp.int32, (2 * length, length), 1)
    row = jnp.where(row >= length, row - length, row)
    taps = jnp.maximum(RADIUS + 1 - jnp.abs(row - col), 0)
    return taps.astype(jnp.float32).astype(jnp.bfloat16)


def kernel(
    sizes,
    den,
    m1,
    m2,
    fwd,
    adj,
    weight,
    new_den,
    new_m1,
    new_m2,
    physical,
    tail,
    z_taps,
    ubuf,
    xbuf,
    sens,
    fbuf,
    abuf,
    m1buf,
    m2buf,
    stage,
    local_sem,
    y_send,
    y_recv,
    t_send,
    t_recv,
    x_send,
    x_recv,
    s_send,
    s_recv,
):
    n_illum, n_gx, n_gy = sizes
    tile_x, tile_y, depth = den.shape
    sources, _, comps = fwd.shape[:3]
    groups = tile_x // RADIUS
    last = groups - 1
    me = lax.axis_index("illum")
    gx = lax.axis_index("gx")
    gy = lax.axis_index("gy")
    odd = lax.rem(gx, 2)
    even = 1 - odd
    reach = tile_x - RADIUS
    starts = [even * (reach - 2 * RADIUS * j) + RADIUS * j for j in range(groups)]
    own = pl.ds(RADIUS, tile_y)

    pair = gx + even - odd
    beyond = gx - even + odd
    has_pair = jnp.logical_and(pair >= 0, pair < n_gx)
    has_beyond = jnp.logical_and(beyond >= 0, beyond < n_gx)
    pair = jnp.clip(pair, 0, n_gx - 1)
    beyond = jnp.clip(beyond, 0, n_gx - 1)
    y_there = (gy > 0, gy < n_gy - 1)
    y_at = (jnp.maximum(gy - 1, 0), jnp.minimum(gy + 1, n_gy - 1))
    y_device = [{"gy": at} for at in y_at]
    c_there = [jnp.logical_and(has_beyond, there) for there in y_there]
    c_device = [{"gx": beyond, "gy": at} for at in y_at]
    others = [{"illum": lax.rem(me + k, n_illum)} for k in range(1, n_illum)]

    barrier = pltpu.get_barrier_semaphore()
    greeted = [
        (y_there[0], y_device[0]),
        (y_there[1], y_device[1]),
        (has_pair, {"gx": pair}),
        (has_beyond, {"gx": beyond}),
        (c_there[0], c_device[0]),
        (c_there[1], c_device[1]),
    ]
    for device in others:
        pl.semaphore_signal(barrier, inc=1, device_id=device, device_id_type=MESH)

    for there, device in greeted:

        @pl.when(there)
        def _(device=device):
            pl.semaphore_signal(barrier, inc=1, device_id=device, device_id_type=MESH)


    loads = {}

    def load(name, src, dst):
        copy = pltpu.make_async_copy(src, dst, local_sem.at[len(loads)])
        copy.start()
        loads[name] = copy

    for j in range(groups):
        part = pl.ds(starts[j], RADIUS)
        load(("f", j), fwd.at[:, :, :, part], fbuf.at[:, :, :, part])
        load(("a", j), adj.at[:, :, :, part], abuf.at[:, :, :, part])
    load("d", den, ubuf.at[0, pl.ds(0, tile_x), own])
    load("m1", m1, m1buf)
    load("m2", m2, m2buf)

    for there, land in ((y_there[0], 0), (y_there[1], RADIUS + tile_y)):

        @pl.when(jnp.logical_not(there))
        def _(land=land):
            for r in range(ROUNDS):
                ubuf[r, :, pl.ds(land, RADIUS)] = jnp.zeros(
                    (tile_x + RADIUS, RADIUS, depth), jnp.float32
                )

    pair_land = even * (tile_x + RADIUS)
    beyond_land = odd * (tile_x + RADIUS)
    for there, land in ((has_pair, pair_land), (has_beyond, beyond_land)):

        @pl.when(jnp.logical_not(there))
        def _(land=land):
            for r in range(ROUNDS):
                xbuf[r, pl.ds(land, RADIUS)] = jnp.zeros(
                    (RADIUS, tile_y, depth), jnp.float32
                )

    tail_at = {last: RADIUS, last - 1: 2 * RADIUS * even, groups: 2 * RADIUS * odd}

    @pl.when(jnp.logical_not(has_beyond))
    def _():
        tail[pl.ds(tail_at[groups], RADIUS)] = jnp.zeros(
            (RADIUS, tile_y, depth), jnp.float32
        )

    z_taps[...] = depth_matrix(depth)

    peers = jnp.int32(len(others))
    for there, _ in greeted:
        peers = peers + there.astype(jnp.int32)
    pl.semaphore_wait(barrier, peers)

    sent_rows = (RADIUS, tile_y)
    landing = (RADIUS + tile_y, 0)

    def rows_of(r, j, low, n, source):
        part = pl.ds(starts[j], RADIUS)
        if source is None:
            return ubuf.at[r, part, pl.ds(low, n)]
        return source.at[part, pl.ds(low - RADIUS, n)]

    def y_copy(r, d, j, source=None):
        return pltpu.make_async_remote_copy(
            src_ref=rows_of(r, j, sent_rows[d], RADIUS, source),
            dst_ref=ubuf.at[r, pl.ds(starts[j], RADIUS), pl.ds(landing[d], RADIUS)],
            send_sem=y_send.at[r, d, j],
            recv_sem=y_recv.at[r, d, j],
            device_id=y_device[d],
            device_id_type=MESH,
        )

    def corner_copy(r, d, source=None):
        return pltpu.make_async_remote_copy(
            src_ref=rows_of(r, last, sent_rows[d], RADIUS, source),
            dst_ref=ubuf.at[r, pl.ds(tile_x, RADIUS), pl.ds(landing[d], RADIUS)],
            send_sem=t_send.at[r, d],
            recv_sem=t_recv.at[r, d],
            device_id=c_device[d],
            device_id_type=MESH,
        )

    def beyond_copy(r, source=None):
        return pltpu.make_async_remote_copy(
            src_ref=rows_of(r, last, RADIUS, tile_y, source),
            dst_ref=ubuf.at[r, pl.ds(tile_x, RADIUS), own],
            send_sem=t_send.at[r, 2],
            recv_sem=t_recv.at[r, 2],
            device_id={"gx": beyond},
            device_id_type=MESH,
        )

    def pair_copy(r, land):
        return pltpu.make_async_remote_copy(
            src_ref=xbuf.at[r, pl.ds(RADIUS + starts[0], RADIUS)],
            dst_ref=xbuf.at[r, pl.ds(land, RADIUS)],
            send_sem=x_send.at[r],
            recv_sem=x_recv.at[r],
            device_id={"gx": pair},
            device_id_type=MESH,
        )

    def s_copy(k, j, slot):
        part = pl.ds(starts[j], RADIUS)
        return pltpu.make_async_remote_copy(
            src_ref=sens.at[me, part],
            dst_ref=sens.at[slot, part],
            send_sem=s_send.at[k, j],
            recv_sem=s_recv.at[k, j],
            device_id=others[k],
            device_id_type=MESH,
        )

    def send(r, j, source=None):
        if j == last:
            for d in (0, 1):

                @pl.when(c_there[d])
                def _(d=d):
                    corner_copy(r, d, source).start()

        for d in (0, 1):

            @pl.when(y_there[d])
            def _(d=d):
                y_copy(r, d, j, source).start()

        if j == last:

            @pl.when(has_beyond)
            def _():
                beyond_copy(r, source).start()

    for j in (0, 1):
        send(0, j, den)

    for j in range(groups):
        if j == 1:
            for i in (last, *range(2, last)):
                send(0, i, den)
        loads["f", j].wait()
        loads["a", j].wait()
        for i in range(RADIUS):
            q = starts[j] + i
            total = None
            for s in range(sources):
                real = None
                for c in range(comps):
                    a = fbuf[s, 0, c, q].astype(jnp.float32) * abuf[s, 0, c, q].astype(
                        jnp.float32
                    )
                    b = fbuf[s, 1, c, q].astype(jnp.float32) * abuf[s, 1, c, q].astype(
                        jnp.float32
                    )
                    real = (a - b) if real is None else real + (a - b)
                term = weight[s] * real
                total = term if total is None else total + term
            sens[me, q] = total
        if j >= LATE_FROM:

            @pl.when(odd == 0)
            def _(j=j):
                for k in range(len(others)):
                    s_copy(k, j, me).start()

        else:
            for k in range(len(others)):
                s_copy(k, j, me).start()

    def taps(ref, step, n):
        one, two, three, four, five = (
            ref[:, pl.ds(step * k, n)] for k in range(5)
        )
        return (one + five) + 2.0 * (two + four) + 3.0 * three

    def store(r, out, j, total):
        if r == ROUNDS - 1 and j in tail_at:
            tail[pl.ds(tail_at[j], RADIUS)] = total
        if r < ROUNDS - 1 or j <= last:
            xbuf[r, pl.ds(out, RADIUS)] = total

    def filter_rows(r, start, out, j):
        near = pl.ds(0, tile_y + 12)
        stage[:, near] = taps(ubuf.at[r, pl.ds(start, RADIUS)], 1, tile_y + 12)
        total = taps(stage, 3, tile_y)
        store(r, out, j, total)

    def y_filter(r, j):
        for d, there in ((0, y_there[1]), (1, y_there[0])):

            @pl.when(there)
            def _(d=d):
                y_copy(r, d, j).wait_recv()

        if r == ROUNDS - 1 and 0 < j < last:
            return
        for i in range(1, last) if r == ROUNDS - 1 and j == last else ():
            filter_rows(r, starts[i], RADIUS + starts[i], i)
        filter_rows(r, starts[j], RADIUS + starts[j], j)
        if j == 0:

            @pl.when(has_pair)
            def _():
                pair_copy(r, odd * (tile_x + RADIUS)).start()

    def pair_arrive(r):
        @pl.when(has_pair)
        def _():
            pair_copy(r, pair_land).wait_recv()

    def beyond_filter(r):
        for d in (0, 1):

            @pl.when(c_there[1 - d])
            def _(d=d):
                corner_copy(r, d).wait_recv()

        @pl.when(has_beyond)
        def _():
            beyond_copy(r).wait_recv()
            filter_rows(r, tile_x, beyond_land, groups)

    def xz_filter(r, j):
        return xz_rows(xbuf[r, pl.ds(starts[j], 3 * RADIUS)], z_taps[...])

    def chain(j, filtered):
        part = pl.ds(starts[j], RADIUS)
        for k in range(len(others)):
            s_copy(k, j, lax.rem(me + n_illum - 1 - k, n_illum)).wait_recv()
        total = sens[0, part]
        for e in range(1, n_illum):
            total = total + sens[e, part]
        inner = jnp.tanh(SHARPNESS * (filtered - THRESHOLD))
        ubuf[1, part, own] = total * (SHARPNESS * (1.0 - inner * inner) * (1.0 / SCALE))
        send(1, j)

    def update(j, gradient):
        part = pl.ds(starts[j], RADIUS)
        one = 0.9 * m1buf[part] + 0.1 * gradient
        two = 0.999 * m2buf[part] + 0.001 * gradient * gradient
        step = one * FIRST_FIX / (jnp.sqrt(two * SECOND_FIX) + 1e-08)
        value = jnp.clip(ubuf[0, part, own] - 0.05 * step, 0.0, 1.0)
        ubuf[2, part, own] = value
        send(2, j)
        new_m1[part] = one
        new_m2[part] = two
        new_den[part] = value

    def finish(j, value):
        part = pl.ds(starts[j], RADIUS)
        physical[part] = project(value)

    def drain(r):
        source = den if r == 0 else None
        for d in (0, 1):

            @pl.when(y_there[d])
            def _(d=d):
                for j in range(groups):
                    y_copy(r, d, j, source).wait_send()

            @pl.when(c_there[d])
            def _(d=d):
                corner_copy(r, d, source).wait_send()

        @pl.when(has_beyond)
        def _():
            beyond_copy(r, source).wait_send()

        @pl.when(has_pair)
        def _():
            pair_copy(r, odd * (tile_x + RADIUS)).wait_send()

    def drain_early():
        for j in range(groups):
            for k in range(len(others)):
                s_copy(k, j, me).wait_send()
        for r in range(ROUNDS - 1):
            drain(r)

    loads["d"].wait()
    steps = plan(groups)
    for r, point in enumerate((chain, update, finish)):
        if r == 1:
            loads["m1"].wait()
            loads["m2"].wait()
        for step, j in steps[r]:
            if step == "y":
                y_filter(r, j)
            elif step == "pair":
                pair_arrive(r)
            elif step == "beyond":
                if r == ROUNDS - 1:
                    drain_early()
                beyond_filter(r)
            elif step == "late":

                @pl.when(odd == 1)
                def _(late=(range(1, 3), range(3, groups))[j]):
                    for j in late:
                        for k in range(len(others)):
                            s_copy(k, j, me).start()

            elif step == "middle":
                inner = xbuf[r, pl.ds(RADIUS, tile_x)]
                physical[pl.ds(RADIUS, tile_x - 2 * RADIUS)] = project(
                    xz_rows(inner, z_taps[...])
                )
            elif r < ROUNDS - 1 or j < last:
                point(j, xz_filter(r, j))

    drain(ROUNDS - 1)


def export(a, b, c, d, tail, z_taps, a_out, b_out, c_out, d_out, edge, sem):
    tile_x = d.shape[0]
    even = 1 - lax.rem(lax.axis_index("gx"), 2)
    done = pl.ds(RADIUS * even, tile_x - RADIUS)
    copies = [
        pltpu.make_async_copy(src, dst, sem.at[i])
        for i, (src, dst) in enumerate(
            ((d.at[done], d_out.at[done]), (a, a_out), (b, b_out), (c, c_out))
        )
    ]
    for copy in copies:
        copy.start()
    edge[...] = project(xz_rows(tail[...], z_taps[...]))
    final = pltpu.make_async_copy(
        edge, d_out.at[pl.ds((tile_x - RADIUS) * (1 - even), RADIUS)], sem.at[4]
    )
    final.start()
    for copy in (*copies, final):
        copy.wait()


def shards(sizes, density, moment_one, moment_two, forward_field, adjoint_field, objective_weight):
    tile_x, tile_y, depth = density.shape
    n_illum = sizes[0]
    tile = jax.ShapeDtypeStruct(density.shape, jnp.float32)
    f32 = jnp.float32
    far = max(n_illum - 1, 1)
    groups = tile_x // RADIUS
    arguments = [
        pltpu.with_memory_space_constraint(x, pltpu.HBM)
        for x in (density, moment_one, moment_two, forward_field, adjoint_field)
    ]
    results = pl.pallas_call(
        functools.partial(kernel, sizes),
        out_shape=(pltpu.VMEM(density.shape, f32),) * 4
        + (
            pltpu.VMEM((3 * RADIUS, tile_y, depth), f32),
            pltpu.VMEM((2 * depth, depth), jnp.bfloat16),
        ),
        in_specs=[pl.BlockSpec(memory_space=pltpu.HBM)] * 5
        + [pl.BlockSpec(memory_space=pltpu.SMEM)],
        out_specs=(pl.BlockSpec(memory_space=pltpu.VMEM),) * 6,
        scratch_shapes=[
            pltpu.VMEM(
                (ROUNDS, tile_x + RADIUS, tile_y + 2 * RADIUS, depth), f32
            ),
            pltpu.VMEM((ROUNDS, tile_x + 2 * RADIUS, tile_y, depth), f32),
            pltpu.VMEM((n_illum, tile_x, tile_y, depth), f32),
            pltpu.VMEM(forward_field.shape, forward_field.dtype),
            pltpu.VMEM(adjoint_field.shape, adjoint_field.dtype),
            pltpu.VMEM(density.shape, f32),
            pltpu.VMEM(density.shape, f32),
            pltpu.VMEM((RADIUS, tile_y + 2 * RADIUS, depth), f32),
            pltpu.SemaphoreType.DMA((2 * groups + 3,)),
            pltpu.SemaphoreType.DMA((ROUNDS, 2, groups)),
            pltpu.SemaphoreType.DMA((ROUNDS, 2, groups)),
            pltpu.SemaphoreType.DMA((ROUNDS, 3)),
            pltpu.SemaphoreType.DMA((ROUNDS, 3)),
            pltpu.SemaphoreType.DMA((ROUNDS,)),
            pltpu.SemaphoreType.DMA((ROUNDS,)),
            pltpu.SemaphoreType.DMA((far, groups)),
            pltpu.SemaphoreType.DMA((far, groups)),
        ],
        compiler_params=pltpu.CompilerParams(
            collective_id=0, has_side_effects=True, vmem_limit_bytes=48 << 20
        ),
        name="design_update",
    )(*arguments, objective_weight)
    return pl.pallas_call(
        export,
        out_shape=(tile,) * 4,
        in_specs=[pl.BlockSpec(memory_space=pltpu.VMEM)] * 6,
        out_specs=(pl.BlockSpec(memory_space=pl.ANY),) * 4,
        scratch_shapes=[
            pltpu.VMEM((RADIUS, tile_y, depth), f32),
            pltpu.SemaphoreType.DMA((5,)),
        ],
        compiler_params=pltpu.CompilerParams(vmem_limit_bytes=4 << 20),
        name="export_results",
    )(*results)


def solution(mesh):
    field = P("illum", None, None, "gx", "gy", None)
    tile = P("gx", "gy", None)
    sizes = (mesh.shape["illum"], mesh.shape["gx"], mesh.shape["gy"])
    return jax.shard_map(
        functools.partial(shards, sizes),
        mesh=mesh,
        in_specs=(tile, tile, tile, field, field, P("illum")),
        out_specs=(tile,) * 4,
        check_vma=False,
    )
```
